512 devices in a mesh: dp: 128 (over y, z, core), cent: 4 (over x).
Axes of the slice: x: 4, y: 8, z: 8, core: 2. Of those that a mesh axis runs over, the one named last changes fastest.
Arguments:
- frames: bfloat16 [524288, 1024], P(('dp', 'cent')), may hold values from -6 to 6
- video_length: int32 [512, 128], P(('dp', 'cent')), may hold values from 1 to 16, 1024 in all within a row
- video_owner: int32 [512, 128], P(('dp', 'cent')), may hold values from 0 to 127, as said below
- video_cluster: int32 [512, 128], P(('dp', 'cent')), may hold values from 0 to 255
- frame_code: int32 [524288], P(('dp', 'cent')), may hold values from 0 to 8191, as said below
- old_coarse: bfloat16 [32768, 1024], P('dp'), may hold values from -6 to 6
- old_codes: float32 [8192, 1024], P(('dp', 'cent')), may hold values from -6 to 6
Outputs:
- new_coarse: float32 [32768, 1024], P(('dp', 'cent'))
- new_codes: float32 [8192, 1024], P(('dp', 'cent'))
The draws below stay inside these ranges and needn't reach their ends.
Inputs may be any that keep to these rules, and one draw needn't show every extreme that they name: `video_owner`: each device's row of 128 videos names one index of dp at most 2 times; in every draw some index of dp is named exactly 2 times in every device's row. `frame_code`: among each device's 1024 frames at most 16 have codes in one block of 64 codes (codes b * 64 to (b + 1) * 64 - 1); in every draw some block gets exactly 16 from every device.
All inputs are finite; a program needn't handle non-finite values.
Results may differ from the reference program's by a relative error of at most 0.0015.
Values may be sent and summed in bfloat16 or wider, within the bound.
A program may use at most 64 MiB of HBM per device.

```python
import math
import jax
import jax.numpy as jnp
import numpy as np
from jax import lax

D = 1024
FR_DEV = 1024
MAXLEN = 16
KC_DEV = 256
KR_DEV = 64
VID_DEV = 128
KC = 32768
KR = 8192
CAPV = 2
CAPC = 16
FRAMES = 524288
N_DP = 128
N_CENT = 4
DEVICES = 512


def spread_block(block_key, item_total, targets, capacity, forced):
    first_key, second_key = jax.random.split(block_key)
    free_places = jax.random.permutation(first_key, (targets - 1) * capacity)[:item_total - capacity]
    other_targets = (free_places // capacity).astype(jnp.int32)
    other_targets = other_targets + (other_targets >= forced).astype(jnp.int32)
    chosen = jnp.concatenate([jnp.full((capacity,), forced, jnp.int32), other_targets])
    return jax.random.permutation(second_key, chosen)


def route_blocks(base_key, item_total, capacity):
    forced = jax.random.randint(jax.random.fold_in(base_key, 1), (), 0, N_DP).astype(jnp.int32)
    block_keys = jax.random.split(jax.random.fold_in(base_key, 2), N_DP * N_CENT)
    return jax.vmap(lambda block_key: spread_block(block_key, item_total, N_DP, capacity, forced))(block_keys)


def draw_video_owner(key, part):
    return route_blocks(jax.random.fold_in(key, 31), VID_DEV, CAPV).astype(jnp.int32)


def draw_frame_code(key, part):
    owners = route_blocks(jax.random.fold_in(key, 47), FR_DEV, CAPC)
    offsets = jax.random.randint(jax.random.fold_in(key, 53), owners.shape, 0, KR_DEV)
    return (owners * KR_DEV + offsets).astype(jnp.int32).reshape(-1)


def touch_ends(array, rng, least, top_value):
    place = [jax.random.randint(jax.random.fold_in(rng, axis), (), 0, length) for axis, length in enumerate(array.shape)]
    widest = array.shape.index(max(array.shape))
    beside = place[:widest] + [(place[widest] + 1) % array.shape[widest]] + place[widest + 1:]
    return array.at[tuple(place)].set(least).at[tuple(beside)].set(top_value)


def block_levels(stream_key, extent, cuts, smallest, largest):
    loudness = 1.0
    for axis_at, shards_of in cuts:
        heights = jax.random.uniform(jax.random.fold_in(jax.random.fold_in(stream_key, 6), axis_at), (shards_of,), jnp.float32, smallest / len(cuts), largest / len(cuts))
        loudness = loudness * jnp.repeat(jnp.exp(heights), extent[axis_at] // shards_of).reshape((-1,) + (1,) * (len(extent) - 1 - axis_at))
    return loudness


def profile(amount, total, reach, skew):
    weights = [(1 << 20) // math.isqrt(rank ** skew) + 1 for rank in range(2, amount + 1)]
    spare, given = total - reach - (amount - 1), [1] * (amount - 1)
    while spare > 0:
        candidates = [i for i in range(amount - 1) if given[i] < reach]
        whole, remaining = sum([weights[i] for i in candidates]), spare
        for i in candidates:
            more = min(reach - given[i], max(1, remaining * weights[i] // whole), spare)
            given[i] = given[i] + more
            spare = spare - more
    return np.array([reach] + given)


def uneven_parts(key, amount, total, reach, lean):
    if amount == 2:
        one = jax.random.randint(key, (), max(1, total - reach), min(reach, total - 1) + 1)
        return jnp.stack([one, total - one])
    sizes = jnp.asarray(profile(amount, total, reach, lean), jnp.int32)
    twos = (amount - 1) // 2
    source_of, taker = sizes[1:1 + 2 * twos:2], sizes[2:2 + 2 * twos:2]
    margin = jnp.minimum(source_of - 1, reach - taker)
    moved = jax.random.randint(jax.random.fold_in(key, 1), (twos,), 0, 1 << 20) % (margin + 1)
    sizes = sizes.at[1:1 + 2 * twos:2].set(source_of - moved).at[2:2 + 2 * twos:2].set(taker + moved)
    return sizes[jax.random.permutation(jax.random.fold_in(key, 2), amount)]


def gaussian(rng, dims, scale, most, cuts=(), kind=jnp.bfloat16):
    entries = scale * jax.random.normal(rng, dims, jnp.float32)
    if cuts:
        entries = entries * block_levels(rng, dims, cuts, -0.22, 0.18)
    return jnp.clip(entries, -most, most).astype(kind)


def setup_inputs(seed: int = 0) -> dict:
    arg_keys = jax.random.split(jax.random.key(seed), 8)
    frames = gaussian(arg_keys[0], (FRAMES, D), 1.0, 6.0, ((0, 512),))
    video_length = jax.vmap(lambda own: uneven_parts(own, VID_DEV, FR_DEV, MAXLEN, 2))(jax.random.split(arg_keys[1], DEVICES)).reshape((DEVICES, VID_DEV)).astype(jnp.int32)
    video_owner = draw_video_owner(jax.random.fold_in(arg_keys[7], 71), 0)
    video_cluster = touch_ends(jax.random.randint(arg_keys[3], (DEVICES, VID_DEV), 0, KC_DEV), jax.random.fold_in(arg_keys[3], 1), 0, KC_DEV - 1).astype(jnp.int32)
    frame_code = draw_frame_code(jax.random.fold_in(arg_keys[7], 71), 0)
    old_coarse = gaussian(arg_keys[5], (KC, D), 1.0, 6.0, ((0, 128),))
    old_codes = gaussian(arg_keys[6], (KR, D), 1.0, 6.0, ((0, 512),), jnp.float32)
    return dict(frames=frames, video_length=video_length, video_owner=video_owner, video_cluster=video_cluster, frame_code=frame_code, old_coarse=old_coarse, old_codes=old_codes)


code_prior = 16.0


def reference(frames, video_length, video_owner, video_cluster, frame_code, old_coarse, old_codes):
    blocks = N_DP * N_CENT
    video_ends = jnp.cumsum(video_length, axis=1)
    position = jnp.arange(FR_DEV, dtype=jnp.int32)
    local_video = jax.vmap(lambda ends_row: jnp.searchsorted(ends_row, position, side="right"))(video_ends).astype(jnp.int32)
    frame_blocks = frames.reshape(blocks, FR_DEV, D)

    def pool_block(packed):
        frame_rows, local_index, lengths = packed
        totals = jax.ops.segment_sum(frame_rows.astype(jnp.float32), local_index, num_segments=VID_DEV)
        return (totals / lengths[:, None].astype(jnp.float32)).astype(jnp.bfloat16)

    pooled = lax.map(pool_block, (frame_blocks, local_video, video_length))
    coarse_ids = (video_owner * KC_DEV + video_cluster).astype(jnp.int32)
    flat_ids = coarse_ids.reshape(-1)
    coarse_sum = jax.ops.segment_sum(pooled.reshape(-1, D).astype(jnp.float32), flat_ids, num_segments=KC)
    coarse_count = jax.ops.segment_sum(jnp.ones(flat_ids.shape, jnp.float32), flat_ids, num_segments=KC)
    new_coarse = (coarse_sum + old_coarse.astype(jnp.float32)) / (coarse_count[:, None] + 1.0)
    anchors = new_coarse.astype(jnp.bfloat16)
    code_blocks = frame_code.reshape(blocks, FR_DEV)

    def add_codes(state, packed):
        frame_rows, local_index, block_ids, code_ids = packed
        frame_coarse = block_ids[local_index]
        residual = (frame_rows.astype(jnp.float32) - anchors[frame_coarse].astype(jnp.float32)).astype(jnp.bfloat16)
        totals, counts = state
        totals = totals + jax.ops.segment_sum(residual.astype(jnp.float32), code_ids, num_segments=KR)
        counts = counts + jax.ops.segment_sum(jnp.ones(code_ids.shape, jnp.float32), code_ids, num_segments=KR)
        return (totals, counts), None

    initial = (jnp.zeros((KR, D), jnp.float32), jnp.zeros((KR,), jnp.float32))
    results = lax.scan(add_codes, initial, (frame_blocks, local_video, coarse_ids, code_blocks))
    code_sum, code_count = results[0]
    new_codes = (code_sum + code_prior * old_codes) / (code_count[:, None] + code_prior)
    return new_coarse, new_codes
```

```python
import jax
import jax.numpy as jnp
from jax import lax
from jax.experimental import pallas as pl
from jax.experimental.pallas import tpu as pltpu
from jax.sharding import PartitionSpec as P

code_prior = 16.0
NL = 8
NY = 8
NZ = 8
W = 128
F32 = jnp.float32
BF16 = jnp.bfloat16


def iota(shape, dim):
    return lax.broadcasted_iota(jnp.int32, shape, dim).astype(F32)


def hot(condition):
    return jnp.where(condition, 1.0, 0.0).astype(BF16)


def columns(row):
    return jnp.transpose(jnp.broadcast_to(row, (128, 128)))


def dot(a, b):
    return jnp.dot(a, b, preferred_element_type=F32)


def dot_t(a, b):
    return lax.dot_general(a, b, (((1,), (1,)), ((), ())), preferred_element_type=F32)


def kernel(
    frames_ref, length_ref, owner_ref, cluster_ref, code_ref, old_ref, old_codes_ref,
    coarse_out, codes_out,
    frames_v, mine, theirs, pooled, pool_in, old_v,
    meta, metas, both, rows, picks, words,
    send_c, hop_c, got_c, back_0, back_1, back_2,
    note_0, note_1, note_s, note_2, fresh, fresh_in,
    table, table_1, part, part_2, last, last_in, count, count_in, column,
    load_sem, xs, xr, fs, fr, ps, pr, ns, nr, cs, cr, bs, br, ts, tr, es, er,
):
    dp = lax.axis_index("dp")
    x = lax.axis_index("cent")
    c = lax.rem(dp, 2)
    z = lax.rem(lax.div(dp, 2), NZ)
    y = lax.div(dp, 2 * NZ)
    m = x * 2 + c
    here = (y, z)

    def member(d):
        other = lax.rem(m + d, NL)
        return other, {"dp": (y * NZ + z) * 2 + lax.rem(other, 2), "cent": lax.div(other, 2)}

    def on_y(d):
        other = lax.rem(y + d, NY)
        return other, {"dp": (other * NZ + z) * 2 + c, "cent": x}

    def on_z(d):
        other = lax.rem(z + d, NZ)
        return other, {"dp": (y * NZ + other) * 2 + c, "cent": x}

    on = (on_y, on_z)

    def remote(src, dst, send, recv, target):
        copy = pltpu.make_async_remote_copy(
            src_ref=src, dst_ref=dst, send_sem=send, recv_sem=recv,
            device_id=target, device_id_type=pl.DeviceIdType.MESH,
        )
        copy.start()
        return copy

    def local(src, dst, sem):
        copy = pltpu.make_async_copy(src, dst, sem)
        copy.start()
        return copy

    def wait(copies):
        for copy in copies:
            copy.wait()

    def spread(src, dst, send, recv, stage, axis):
        copies = []
        for d in range(1, 8):
            other, target = on[axis](d)
            copies.append(remote(src(other), dst, send.at[stage, d], recv.at[stage, d], target))
        return copies

    barrier = pltpu.get_barrier_semaphore()
    for d in range(1, 8):
        for find in (member, on_y, on_z):
            pl.semaphore_signal(
                barrier, inc=1, device_id=find(d)[1], device_id_type=pl.DeviceIdType.MESH
            )

    my_lanes = pl.ds(pl.multiple_of(m * W, W), W)
    load = local(frames_ref, frames_v, load_sem.at[0])
    load_mine = local(frames_ref.at[:, my_lanes], theirs.at[m], load_sem.at[1])
    load_old = local(old_ref.at[:, my_lanes], old_v.at[c], load_sem.at[2])

    sub128, lane128 = iota((128, 128), 0), iota((128, 128), 1)
    sub64 = iota((64, 128), 0)
    length = length_ref[...].astype(F32)
    through = hot(sub128 <= lane128)
    before = hot(sub128 < lane128)
    ends_row = dot(jnp.broadcast_to(length, (8, 128)).astype(BF16), through)[0:1]
    ends = columns(ends_row)
    lengths = columns(length)
    starts = ends - lengths
    pieces = []
    for a in range(8):
        position = lane128 + 128.0 * a
        pieces.append(hot(jnp.logical_and(position >= starts, position < ends)))
        meta[16 + a : 17 + a, :] = jnp.sum(
            jnp.where(ends <= position, 1.0, 0.0), axis=0, keepdims=True
        )
    of_video = jnp.concatenate(pieces, axis=1)

    owner_int = owner_ref[...]
    owner = owner_int.astype(F32)
    same = jnp.logical_and(columns(owner) == owner, sub128 < lane128)
    repeat = jnp.sum(jnp.where(same, 1.0, 0.0), axis=0, keepdims=True)
    half = jnp.bitwise_and(owner_int, 1)
    to_y = jnp.right_shift(owner_int, 4)
    to_z = jnp.bitwise_and(jnp.right_shift(owner_int, 1), NZ - 1)
    place = jnp.where(half == 0, to_y * NZ + to_z, to_z * NY + to_y)
    meta[32:33, :] = (half * 1024 + place * 16).astype(F32) + repeat
    meta[33:34, :] = cluster_ref[...].astype(F32) + 1.0
    meta[34:35, :] = place.astype(F32)
    meta[35:36, :] = repeat
    meta[36:37, :] = half.astype(F32)
    meta[37:40, :] = jnp.zeros((3, 128), F32)

    codes = code_ref[...]
    line_of = jnp.right_shift(codes, 7).astype(F32)
    in_line = jnp.bitwise_and(codes, 127).astype(F32)
    ones = jnp.ones((128, 128), BF16)
    seen = jnp.zeros((64, 128), F32)
    histogram = jnp.zeros((64, 128), F32)
    for a in range(8):
        match = hot(line_of[a : a + 1] == sub64)
        rank = jnp.sum(
            match.astype(F32) * (dot(match, before) + seen), axis=0, keepdims=True
        )
        meta[a : a + 1, :] = line_of[a : a + 1] * 32.0 + rank
        seen = seen + dot(match, ones)
        histogram = histogram + dot_t(match, hot(in_line[a : a + 1] == sub128))
    meta[8:16, :] = in_line
    meta[24:32, :] = line_of
    metas[pl.ds(m, 1)] = meta[...].reshape(1, 40, 128)
    for j in range(8):
        note_0[0, j, 0:8, :] = histogram[8 * j : 8 * j + 8]
        note_0[1, j, 0:8, :] = jnp.zeros((8, 128), F32)

    pl.semaphore_wait(barrier, 21)
    x_copies, f_copies, p_copies = [], [], []
    for d in range(1, 8):
        other, target = member(d)
        x_copies.append(remote(meta, metas.at[m], xs.at[d], xr.at[d], target))
    partner = lax.rem(c + 1, 2)
    old_copy = remote(
        old_ref.at[:, pl.ds(pl.multiple_of((x * 2 + partner) * W, W), W)],
        old_v.at[c], xs.at[0], xr.at[0],
        {"dp": (y * NZ + z) * 2 + partner, "cent": x},
    )
    load.wait()
    for j in range(8):
        part_sum = dot(of_video, frames_v[:, 128 * j : 128 * j + 128])
        pooled[j] = (part_sum / lengths).astype(BF16)
    for d in range(1, 8):
        other, target = member(d)
        p_copies.append(
            remote(pooled.at[other], pool_in.at[m], ps.at[d], pr.at[d], target)
        )
    for d in range(1, 8):
        other, target = member(d)
        lanes = pl.ds(pl.multiple_of(other * W, W), W)
        f_copies.append(
            remote(frames_ref.at[:, lanes], theirs.at[m], fs.at[d], fr.at[d], target)
        )
    pool_in[pl.ds(m, 1)] = pooled[pl.ds(m, 1)]

    wait(x_copies)
    note = [jnp.zeros((64, 128), F32), jnp.zeros((64, 128), F32)]
    for s in range(NL):
        info = metas[s, 32:40, :]
        value = info[1:2]
        at = jnp.where(info[2:3] == sub64, value, 0.0)
        for h in range(2):
            chosen = jnp.where(info[4:5] == float(h), at, 0.0).astype(BF16)
            lane = hot(info[3:4] + (here[h] * 16 + 2 * s).astype(F32) == sub128)
            note[h] = note[h] + dot_t(chosen, lane)
    for h in range(2):
        for j in range(8):
            note_0[h, j, 8:16, :] = note[h][8 * j : 8 * j + 8]
    n_copies = []
    for h in range(2):
        n_copies += spread(lambda o: note_0.at[h, o], note_1.at[h, here[h]], ns, nr, h, h)
        note_1[h, pl.ds(here[h], 1)] = note_0[h, pl.ds(here[h], 1)]

    wait(p_copies)
    sub256 = iota((256, 128), 0)

    def fill(chunk, carry):
        shift = (chunk * 256).astype(F32)
        pick = jnp.concatenate(
            [hot(metas[s, 32:33, :] + 2.0 * s - shift == sub256) for s in range(NL)], axis=1
        )
        filled = dot(pick, pool_in[...].reshape(1024, W))
        send_c[pl.ds(chunk * 16, 16)] = filled.astype(BF16).reshape(16, 16, W)
        return carry

    lax.fori_loop(0, 8, fill, 0)
    c_copies = []
    for h in range(2):
        c_copies += spread(
            lambda o: send_c.at[pl.ds(64 * h + 8 * o, 8)], hop_c.at[h, here[h]], cs, cr, h, h
        )
        hop_c[h, pl.ds(here[h], 1)] = send_c[pl.ds(64 * h + 8 * here[h], 8)].reshape(1, 8, 16, W)

    wait(n_copies)
    for h in range(2):
        note_s[h] = jnp.sum(note_1[h], axis=0)
    n_copies = []
    for h in range(2):
        n_copies += spread(
            lambda o: note_s.at[h], note_2.at[h, here[1 - h]], ns, nr, 2 + h, 1 - h
        )
        note_2[h, pl.ds(here[1 - h], 1)] = note_s[h].reshape(1, 16, 128)

    def take(d):
        s = lax.rem(m + NL - d, NL)
        for a in range(8):
            both[128 * a : 128 * a + 128, W:] = hot(
                columns(metas[s, 16 + a : 17 + a, :]) == lane128
            )
        both[:, :W] = theirs[s]

        def chunk_of(chunk, carry):
            shift = (chunk * 256).astype(F32)
            pick = jnp.concatenate(
                [hot(metas[s, a : a + 1, :] - shift == sub256) for a in range(8)], axis=1
            )
            out = dot(pick, both[...]).astype(BF16)
            rows[s, pl.ds(chunk * 8, 8)] = out[:, :W].reshape(8, 32, W)
            picks[s, pl.ds(chunk * 8, 8)] = out[:, W:].reshape(8, 32, W)
            return carry

        lax.fori_loop(0, 8, chunk_of, 0)

    def arrive(d):
        if d == 0:
            load_mine.wait()
        else:
            f_copies[d - 1].wait()
        take(d)

    def word(s, carry):
        total = jnp.zeros((64, 128), F32)
        offset = (lax.rem(s, 4) * 32).astype(F32)
        for a in range(8):
            line = metas[s, 24 + a : 25 + a, :]
            rank = metas[s, a : a + 1, :] - 32.0 * line + offset
            value = metas[s, 8 + a : 9 + a, :] + 1.0
            total = total + dot_t(
                jnp.where(line == sub64, value, 0.0).astype(BF16), hot(rank == sub128)
            )
        group = pl.ds(lax.div(s, 4), 1)
        words[group] = words[group] + total.reshape(1, 64, 128)
        return carry

    arrive(0)
    arrive(1)

    wait(c_copies)
    c_copies = []
    for h in range(2):
        c_copies += spread(
            lambda o: hop_c.at[h, :, o], got_c.at[h, here[1 - h]], cs, cr, 2 + h, 1 - h
        )
        got_c[h, pl.ds(here[1 - h], 1)] = hop_c[h, :, pl.ds(here[1 - h], 1)].reshape(1, 8, 16, W)
    words[...] = jnp.zeros((2, 64, 128), F32)
    lax.fori_loop(0, NL, word, 0)
    arrive(2)
    wait(n_copies)
    load_old.wait()
    old_copy.wait()
    wait(c_copies)

    sub8 = iota((8, 128), 0)
    b_copies, v_copies = [], []
    for h in range(2):
        mask = sub8 == here[1 - h].astype(F32)
        ids = [
            jnp.sum(jnp.where(mask, note_2[h, j, 8:16, :], 0.0), axis=0, keepdims=True)
            for j in range(8)
        ]
        pick = jnp.concatenate([hot(ids[j] == sub256 + 1.0) for j in range(8)], axis=1)
        total = dot(pick, got_c[h].reshape(1024, W))
        amount = dot(pick, jnp.ones((1024, W), BF16))
        new = (total + old_v[h].astype(F32)) / (amount + 1.0)
        for q in range(4):
            fresh[2 * q + h] = new[64 * q : 64 * q + 64]
        anchor = new.astype(BF16)
        lane256 = iota((128, 256), 1)
        for j in range(8):
            column_of = columns(ids[j])
            back = hot(jnp.concatenate([column_of, column_of], axis=1) == lane256 + 1.0)
            back_0[h, j] = dot(back, anchor).astype(BF16).reshape(8, 16, W)
        b_copies += spread(
            lambda o: back_0.at[h, o], back_1.at[h, here[1 - h]], bs, br, h, 1 - h
        )
        back_1[h, pl.ds(here[1 - h], 1)] = back_0[h, pl.ds(here[1 - h], 1)]
    counts = jnp.zeros((1, 128), F32)
    for j in range(8):
        counts = counts + jnp.sum(
            jnp.where(sub8 == z.astype(F32), note_2[0, j, 0:8, :], 0.0), axis=0, keepdims=True
        )
    count[...] = jnp.broadcast_to(counts, (8, 128))
    count_in[pl.ds(m, 1)] = count[...].reshape(1, 8, 128)
    for d in range(1, 8):
        other, target = member(d)
        v_copies.append(
            remote(fresh.at[other], fresh_in.at[m], es.at[0, d], er.at[0, d], target)
        )
        v_copies.append(
            remote(count, count_in.at[m], es.at[1, d], er.at[1, d], target)
        )
    fresh_in[pl.ds(m, 1)] = fresh[pl.ds(m, 1)]
    arrive(3)
    arrive(4)

    wait(b_copies)
    b_copies = []
    for h in range(2):
        b_copies += spread(
            lambda o: back_1.at[h, :, o], back_2.at[h, here[h]], bs, br, 2 + h, h
        )
        back_2[h, pl.ds(here[h], 1)] = back_1[h, :, pl.ds(here[h], 1)].reshape(1, 8, 16, W)
    arrive(5)
    arrive(6)
    arrive(7)
    wait(b_copies)

    def subtract(s, carry):
        wanted = columns(metas[s, 32:33, :] + (2 * s).astype(F32))
        pick = jnp.concatenate([hot(wanted == lane128 + 128.0 * t) for t in range(16)], axis=1)
        anchor = dot(pick, back_2[...].reshape(2048, W)).astype(BF16)

        def chunk_of(chunk, inner):
            at = pl.ds(chunk * 8, 8)
            near = dot(picks[s, at].reshape(256, W), anchor)
            left = rows[s, at].reshape(256, W).astype(F32) - near
            rows[s, at] = left.astype(BF16).reshape(8, 32, W)
            return inner

        return lax.fori_loop(0, 8, chunk_of, carry)

    lax.fori_loop(0, NL, subtract, 0)

    def tabulate(k, carry):
        pick = jnp.concatenate(
            [hot(words[g, pl.ds(k, 1), :] == sub128 + 1.0) for g in range(2)], axis=1
        )
        sums = dot(pick, rows[:, pl.ds(k, 1)].reshape(256, W)).astype(BF16)
        across = lax.rem(k, 8) * 8 + lax.div(k, 8)
        table[0, pl.ds(k, 1)] = sums[0:64].reshape(1, 64, W)
        table[1, pl.ds(across, 1)] = sums[64:128].reshape(1, 64, W)
        return carry

    lax.fori_loop(0, 64, tabulate, 0)
    t_copies = []
    for h in range(2):
        t_copies += spread(
            lambda o: table.at[h, pl.ds(8 * o, 8)], table_1.at[h, here[h]], ts, tr, h, h
        )
        table_1[h, pl.ds(here[h], 1)] = table[h, pl.ds(8 * here[h], 8)].reshape(1, 8, 64, W)
    wait(v_copies)
    for s in range(NL):
        coarse_out[:, W * s : W * s + W] = fresh_in[s]
    column[...] = columns(jnp.sum(count_in[...], axis=0)[0:1])
    wait(t_copies)

    def gather(j, carry):
        for h in range(2):
            total = jnp.zeros((64, W), F32)
            for i in range(8):
                total = total + table_1[h, i, pl.ds(j, 1)].reshape(64, W).astype(F32)
            part[h, pl.ds(j, 1)] = total.reshape(1, 64, W)
        return carry

    lax.fori_loop(0, 8, gather, 0)
    t_copies = []
    for h in range(2):
        t_copies += spread(
            lambda o: part.at[h, o], part_2.at[h, here[1 - h]], ts, tr, 2 + h, 1 - h
        )
        part_2[h, pl.ds(here[1 - h], 1)] = part[h, pl.ds(here[1 - h], 1)]
    wait(t_copies)
    for h in range(2):
        total = jnp.sum(part_2[h], axis=0)
        for q in range(4):
            last[2 * q + h] = total[16 * q : 16 * q + 16]
    e_copies = []
    for d in range(1, 8):
        other, target = member(d)
        e_copies.append(
            remote(last.at[other], last_in.at[m], es.at[2, d], er.at[2, d], target)
        )
    last_in[pl.ds(m, 1)] = last[pl.ds(m, 1)]
    mine[...] = column[pl.ds(pl.multiple_of(c * 64 + x * 16, 16), 16), :] + code_prior
    wait(e_copies)
    for s in range(NL):
        lanes = slice(W * s, W * s + W)
        codes_out[:, lanes] = (last_in[s] + code_prior * old_codes_ref[:, lanes]) / mine[...]


def body(frames, video_length, video_owner, video_cluster, frame_code, old_coarse, old_codes):
    dma = pltpu.SemaphoreType.DMA
    vmem = pl.BlockSpec(memory_space=pltpu.VMEM)
    hbm = pl.BlockSpec(memory_space=pl.ANY)
    return pl.pallas_call(
        kernel,
        out_shape=(
            jax.ShapeDtypeStruct((64, 1024), F32),
            jax.ShapeDtypeStruct((16, 1024), F32),
        ),
        in_specs=[hbm, vmem, vmem, vmem, vmem, hbm, vmem],
        out_specs=(vmem, vmem),
        scratch_shapes=[
            pltpu.VMEM((1024, 1024), BF16),
            pltpu.VMEM((16, 128), F32),
            pltpu.VMEM((NL, 1024, W), BF16),
            pltpu.VMEM((NL, 128, W), BF16),
            pltpu.VMEM((NL, 128, W), BF16),
            pltpu.VMEM((2, 256, W), BF16),
            pltpu.VMEM((40, 128), F32),
            pltpu.VMEM((NL, 40, 128), F32),
            pltpu.VMEM((1024, 2 * W), BF16),
            pltpu.VMEM((NL, 64, 32, W), BF16),
            pltpu.VMEM((NL, 64, 32, W), BF16),
            pltpu.VMEM((2, 64, 128), F32),
            pltpu.VMEM((128, 16, W), BF16),
            pltpu.VMEM((2, 8, 8, 16, W), BF16),
            pltpu.VMEM((2, 8, 8, 16, W), BF16),
            pltpu.VMEM((2, 8, 8, 16, W), BF16),
            pltpu.VMEM((2, 8, 8, 16, W), BF16),
            pltpu.VMEM((2, 8, 8, 16, W), BF16),
            pltpu.VMEM((2, 8, 16, 128), F32),
            pltpu.VMEM((2, 8, 16, 128), F32),
            pltpu.VMEM((2, 16, 128), F32),
            pltpu.VMEM((2, 8, 16, 128), F32),
            pltpu.VMEM((NL, 64, W), F32),
            pltpu.VMEM((NL, 64, W), F32),
            pltpu.VMEM((2, 64, 64, W), BF16),
            pltpu.VMEM((2, 8, 8, 64, W), BF16),
            pltpu.VMEM((2, 8, 64, W), F32),
            pltpu.VMEM((2, 8, 64, W), F32),
            pltpu.VMEM((NL, 16, W), F32),
            pltpu.VMEM((NL, 16, W), F32),
            pltpu.VMEM((8, 128), F32),
            pltpu.VMEM((NL, 8, 128), F32),
            pltpu.VMEM((128, 128), F32),
            dma((3,)),
            dma((8,)), dma((8,)),
            dma((8,)), dma((8,)),
            dma((8,)), dma((8,)),
            dma((4, 8)), dma((4, 8)),
            dma((4, 8)), dma((4, 8)),
            dma((4, 8)), dma((4, 8)),
            dma((4, 8)), dma((4, 8)),
            dma((3, 8)), dma((3, 8)),
        ],
        compiler_params=pltpu.CompilerParams(
            collective_id=0, has_side_effects=True, vmem_limit_bytes=56 << 20
        ),
    )(
        frames, video_length, video_owner, video_cluster,
        frame_code.reshape(8, 128), old_coarse, old_codes,
    )


def solution(mesh):
    placed = (
        P(("dp", "cent"), None),
        P(("dp", "cent"), None),
        P(("dp", "cent"), None),
        P(("dp", "cent"), None),
        P(("dp", "cent")),
        P("dp", None),
        P(("dp", "cent"), None),
    )
    return jax.shard_map(
        body,
        mesh=mesh,
        in_specs=placed,
        out_specs=(P(("dp", "cent"), None), P(("dp", "cent"), None)),
        check_vma=False,
    )
```

```python
import jax
import jax.numpy as jnp
from jax import lax
from jax.experimental import pallas as pl
from jax.experimental.pallas import tpu as pltpu
from jax.sharding import PartitionSpec as P

code_prior = 16.0
NL = 8
NY = 8
NZ = 8
W = 128
F32 = jnp.float32
BF16 = jnp.bfloat16


def iota(shape, dim):
    return lax.broadcasted_iota(jnp.int32, shape, dim).astype(F32)


def hot(condition):
    return jnp.where(condition, 1.0, 0.0).astype(BF16)


def columns(row):
    return jnp.transpose(jnp.broadcast_to(row, (128, 128)))


def dot(a, b):
    return jnp.dot(a, b, preferred_element_type=F32)


def dot_t(a, b):
    return lax.dot_general(a, b, (((1,), (1,)), ((), ())), preferred_element_type=F32)


def kernel(
    frames_ref, length_ref, owner_ref, cluster_ref, code_ref, old_ref, old_codes_ref,
    coarse_out, codes_out,
    frames_v, mine, theirs, pooled, pool_in, old_v,
    meta, metas, both, rows, picks, rest, words, wants, anchors,
    send_c, hop_c, got_c, back_0, back_1, back_2,
    note_0, note_1, note_s, note_2, fresh, fresh_in,
    table, table_1, part, part_2, last, last_in, count, count_in, column,
    load_sem, xs, xr, fs, fr, ps, pr, ns, nr, cs, cr, bs, br, ts, tr, es, er,
):
    dp = lax.axis_index("dp")
    x = lax.axis_index("cent")
    c = lax.rem(dp, 2)
    z = lax.rem(lax.div(dp, 2), NZ)
    y = lax.div(dp, 2 * NZ)
    m = x * 2 + c
    here = (y, z)

    def member(d):
        other = lax.rem(m + d, NL)
        return other, {"dp": (y * NZ + z) * 2 + lax.rem(other, 2), "cent": lax.div(other, 2)}

    def on_y(d):
        other = lax.rem(y + d, NY)
        return other, {"dp": (other * NZ + z) * 2 + c, "cent": x}

    def on_z(d):
        other = lax.rem(z + d, NZ)
        return other, {"dp": (y * NZ + other) * 2 + c, "cent": x}

    on = (on_y, on_z)

    def remote(src, dst, send, recv, target, start=True):
        copy = pltpu.make_async_remote_copy(
            src_ref=src, dst_ref=dst, send_sem=send, recv_sem=recv,
            device_id=target, device_id_type=pl.DeviceIdType.MESH,
        )
        if start:
            copy.start()
        return copy

    def local(src, dst, sem):
        copy = pltpu.make_async_copy(src, dst, sem)
        copy.start()
        return copy

    def wait(copies):
        for copy in copies:
            copy.wait()

    def spread(src, dst, send, recv, stage, axis):
        copies = []
        for d in range(1, 8):
            other, target = on[axis](d)
            copies.append(remote(src(other), dst, send.at[stage, d], recv.at[stage, d], target))
        return copies

    barrier = pltpu.get_barrier_semaphore()
    for d in range(1, 8):
        for find in (member, on_y, on_z):
            pl.semaphore_signal(
                barrier, inc=1, device_id=find(d)[1], device_id_type=pl.DeviceIdType.MESH
            )

    my_lanes = pl.ds(pl.multiple_of(m * W, W), W)
    load = local(frames_ref, frames_v, load_sem.at[0])
    load_mine = local(frames_ref.at[:, my_lanes], theirs.at[m], load_sem.at[1])
    load_old = local(old_ref.at[:, my_lanes], old_v.at[c], load_sem.at[2])

    sub128, lane128 = iota((128, 128), 0), iota((128, 128), 1)
    sub64 = iota((64, 128), 0)
    length = length_ref[...].astype(F32)
    through = hot(sub128 <= lane128)
    before = hot(sub128 < lane128)
    ends_row = dot(jnp.broadcast_to(length, (8, 128)).astype(BF16), through)[0:1]
    ends = columns(ends_row)
    lengths = columns(length)
    starts = ends - lengths
    pieces = []
    for a in range(8):
        position = lane128 + 128.0 * a
        pieces.append(hot(jnp.logical_and(position >= starts, position < ends)))
        meta[16 + a : 17 + a, :] = jnp.sum(
            jnp.where(ends <= position, 1.0, 0.0), axis=0, keepdims=True
        )
    of_video = jnp.concatenate(pieces, axis=1)

    owner_int = owner_ref[...]
    owner = owner_int.astype(F32)
    same = jnp.logical_and(columns(owner) == owner, sub128 < lane128)
    repeat = jnp.sum(jnp.where(same, 1.0, 0.0), axis=0, keepdims=True)
    half = jnp.bitwise_and(owner_int, 1)
    to_y = jnp.right_shift(owner_int, 4)
    to_z = jnp.bitwise_and(jnp.right_shift(owner_int, 1), NZ - 1)
    place = jnp.where(half == 0, to_y * NZ + to_z, to_z * NY + to_y)
    meta[32:33, :] = (half * 1024 + place * 16).astype(F32) + repeat
    meta[33:34, :] = cluster_ref[...].astype(F32) + 1.0
    meta[34:35, :] = place.astype(F32)
    meta[35:36, :] = repeat
    meta[36:37, :] = half.astype(F32)
    meta[37:40, :] = jnp.zeros((3, 128), F32)

    codes = code_ref[...]
    line_of = jnp.right_shift(codes, 7).astype(F32)
    in_line = jnp.bitwise_and(codes, 127).astype(F32)
    ones = jnp.ones((128, 128), BF16)
    seen = jnp.zeros((64, 128), F32)
    histogram = jnp.zeros((64, 128), F32)
    for a in range(8):
        match = hot(line_of[a : a + 1] == sub64)
        rank = jnp.sum(
            match.astype(F32) * (dot(match, before) + seen), axis=0, keepdims=True
        )
        meta[a : a + 1, :] = line_of[a : a + 1] * 32.0 + rank
        seen = seen + dot(match, ones)
        histogram = histogram + dot_t(match, hot(in_line[a : a + 1] == sub128))
    meta[8:16, :] = in_line
    meta[24:32, :] = line_of
    metas[pl.ds(m, 1)] = meta[...].reshape(1, 40, 128)
    for j in range(8):
        note_0[0, j, 0:8, :] = histogram[8 * j : 8 * j + 8]
        note_0[1, j, 0:8, :] = jnp.zeros((8, 128), F32)

    load.wait()
    for j in range(8):
        part_sum = dot(of_video, frames_v[:, 128 * j : 128 * j + 128])
        pooled[j] = (part_sum / lengths).astype(BF16)
    pl.semaphore_wait(barrier, 21)
    x_copies, f_copies, p_copies = [], [], []
    for d in range(1, 8):
        other, target = member(d)
        x_copies.append(remote(meta, metas.at[m], xs.at[d], xr.at[d], target))
    partner = lax.rem(c + 1, 2)
    old_copy = remote(
        old_ref.at[:, pl.ds(pl.multiple_of((x * 2 + partner) * W, W), W)],
        old_v.at[c], xs.at[0], xr.at[0],
        {"dp": (y * NZ + z) * 2 + partner, "cent": x},
    )
    for d in range(1, 8):
        other, target = member(d)
        p_copies.append(
            remote(pooled.at[other], pool_in.at[m], ps.at[d], pr.at[d], target)
        )
    for d in range(1, 8):
        other, target = member(d)
        lanes = pl.ds(pl.multiple_of(other * W, W), W)
        f_copies.append(
            remote(frames_ref.at[:, lanes], theirs.at[m], fs.at[d], fr.at[d], target)
        )
    pool_in[pl.ds(m, 1)] = pooled[pl.ds(m, 1)]

    wait(x_copies)
    places, values, halves, repeats = [
        [metas[s, i : i + 1, :] for s in range(NL)] for i in (34, 33, 36, 35)
    ]
    note = []
    for h in range(2):
        chosen = [
            jnp.where(
                jnp.logical_and(places[s] == sub64, halves[s] == float(h)), values[s], 0.0
            ).astype(BF16)
            for s in range(NL)
        ]
        lane = [hot(repeats[s] + (here[h] * 16 + 2 * s).astype(F32) == sub128) for s in range(NL)]
        note.append(dot_t(jnp.concatenate(chosen, axis=1), jnp.concatenate(lane, axis=1)))
    for h in range(2):
        for j in range(8):
            note_0[h, j, 8:16, :] = note[h][8 * j : 8 * j + 8]
    n_copies = []
    for h in range(2):
        n_copies += spread(lambda o: note_0.at[h, o], note_1.at[h, here[h]], ns, nr, h, h)
        note_1[h, pl.ds(here[h], 1)] = note_0[h, pl.ds(here[h], 1)]

    wait(p_copies)
    sub256 = iota((256, 128), 0)

    def fill(chunk, carry):
        shift = (chunk * 256).astype(F32)
        pick = jnp.concatenate(
            [hot(metas[s, 32:33, :] + 2.0 * s - shift == sub256) for s in range(NL)], axis=1
        )
        filled = dot(pick, pool_in[...].reshape(1024, W))
        send_c[pl.ds(chunk * 16, 16)] = filled.astype(BF16).reshape(16, 16, W)
        return carry

    lax.fori_loop(0, 8, fill, 0)
    c_copies = []
    for h in range(2):
        c_copies += spread(
            lambda o: send_c.at[pl.ds(64 * h + 8 * o, 8)], hop_c.at[h, here[h]], cs, cr, h, h
        )
        hop_c[h, pl.ds(here[h], 1)] = send_c[pl.ds(64 * h + 8 * here[h], 8)].reshape(1, 8, 16, W)

    wait(n_copies)
    for h in range(2):
        note_s[h] = jnp.sum(note_1[h], axis=0)
    n_copies = []
    for h in range(2):
        n_copies += spread(
            lambda o: note_s.at[h], note_2.at[h, here[1 - h]], ns, nr, 2 + h, 1 - h
        )
        note_2[h, pl.ds(here[1 - h], 1)] = note_s[h].reshape(1, 16, 128)

    def take(d):
        s = lax.rem(m + NL - d, NL)
        for a in range(8):
            both[128 * a : 128 * a + 128, W:] = hot(
                columns(metas[s, 16 + a : 17 + a, :]) == lane128
            )
        both[:, :W] = theirs[s]

        def chunk_of(chunk, carry):
            shift = (chunk * 256).astype(F32)
            pick = jnp.concatenate(
                [hot(metas[s, a : a + 1, :] - shift == sub256) for a in range(8)], axis=1
            )
            out = dot(pick, both[...]).astype(BF16)
            rows[s, pl.ds(chunk * 8, 8)] = out[:, :W].reshape(8, 32, W)
            picks[s, pl.ds(chunk * 8, 8)] = out[:, W:].reshape(8, 32, W)
            return carry

        lax.fori_loop(0, 8, chunk_of, 0)

    def arrive(d):
        if d == 0:
            load_mine.wait()
        else:
            f_copies[d - 1].wait()
        take(d)

    def word(s, carry):
        offset = (lax.rem(s, 4) * 32).astype(F32)
        values, ranks = [], []
        for a in range(8):
            line = metas[s, 24 + a : 25 + a, :]
            rank = metas[s, a : a + 1, :] - 32.0 * line + offset
            value = metas[s, 8 + a : 9 + a, :] + 1.0
            values.append(jnp.where(line == sub64, value, 0.0).astype(BF16))
            ranks.append(hot(rank == sub128))
        total = dot_t(jnp.concatenate(values, axis=1), jnp.concatenate(ranks, axis=1))
        group = pl.ds(lax.div(s, 4), 1)
        words[group] = words[group] + total.reshape(1, 64, 128)
        return carry

    def choose(s, carry):
        wanted = columns(metas[s, 32:33, :] + (2 * s).astype(F32))
        pick = [hot(wanted == lane128 + 128.0 * t) for t in range(16)]
        wants[pl.ds(pl.multiple_of(s * 128, 128), 128), :] = jnp.concatenate(pick, axis=1)
        return carry

    arrive(0)
    words[...] = jnp.zeros((2, 64, 128), F32)
    lax.fori_loop(0, NL, word, 0)
    lax.fori_loop(0, NL, choose, 0)

    wait(c_copies)
    c_copies = []
    for h in range(2):
        c_copies += spread(
            lambda o: hop_c.at[h, :, o], got_c.at[h, here[1 - h]], cs, cr, 2 + h, 1 - h
        )
        got_c[h, pl.ds(here[1 - h], 1)] = hop_c[h, :, pl.ds(here[1 - h], 1)].reshape(1, 8, 16, W)
    arrive(1)
    arrive(2)
    wait(n_copies)
    load_old.wait()
    old_copy.wait()
    wait(c_copies)

    sub8 = iota((8, 128), 0)
    b_copies, v_copies = [], []
    for h in range(2):
        mask = sub8 == here[1 - h].astype(F32)
        ids = [
            jnp.sum(jnp.where(mask, note_2[h, j, 8:16, :], 0.0), axis=0, keepdims=True)
            for j in range(8)
        ]
        pick = jnp.concatenate([hot(ids[j] == sub256 + 1.0) for j in range(8)], axis=1)
        total = dot(pick, got_c[h].reshape(1024, W))
        amount = dot(pick, jnp.ones((1024, W), BF16))
        new = (total + old_v[h].astype(F32)) / (amount + 1.0)
        for q in range(4):
            fresh[2 * q + h] = new[64 * q : 64 * q + 64]
        anchor = new.astype(BF16)
        lane256 = iota((128, 256), 1)
        for j in range(8):
            column_of = columns(ids[j])
            back = hot(jnp.concatenate([column_of, column_of], axis=1) == lane256 + 1.0)
            back_0[h, j] = dot(back, anchor).astype(BF16).reshape(8, 16, W)
        b_copies += spread(
            lambda o: back_0.at[h, o], back_1.at[h, here[1 - h]], bs, br, h, 1 - h
        )
        back_1[h, pl.ds(here[1 - h], 1)] = back_0[h, pl.ds(here[1 - h], 1)]
    counts = jnp.zeros((1, 128), F32)
    for j in range(8):
        counts = counts + jnp.sum(
            jnp.where(sub8 == z.astype(F32), note_2[0, j, 0:8, :], 0.0), axis=0, keepdims=True
        )
    count[...] = jnp.broadcast_to(counts, (8, 128))
    count_in[pl.ds(m, 1)] = count[...].reshape(1, 8, 128)
    for d in range(1, 8):
        other, target = member(d)
        v_copies.append(
            remote(fresh.at[other], fresh_in.at[m], es.at[0, d], er.at[0, d], target)
        )
        v_copies.append(
            remote(count, count_in.at[m], es.at[1, d], er.at[1, d], target)
        )
    fresh_in[pl.ds(m, 1)] = fresh[pl.ds(m, 1)]
    arrive(3)
    arrive(4)
    arrive(5)

    wait(b_copies)
    b_copies = []
    for h in range(2):
        b_copies += spread(
            lambda o: back_1.at[h, :, o], back_2.at[h, here[h]], bs, br, 2 + h, h
        )
        back_2[h, pl.ds(here[h], 1)] = back_1[h, :, pl.ds(here[h], 1)].reshape(1, 8, 16, W)
    arrive(6)
    arrive(7)
    wait(b_copies)

    def read(chunk, carry):
        at = pl.multiple_of(chunk * 256, 256)
        found = dot(wants[pl.ds(at, 256), :], back_2[...].reshape(2048, W))
        anchors[pl.ds(chunk * 2, 2)] = found.astype(BF16).reshape(2, 128, W)
        return carry

    lax.fori_loop(0, 4, read, 0)

    def tabulate(to):
        at = pl.ds(to * 8, 8)
        for s in range(NL):
            near = dot(picks[s, at].reshape(256, W), anchors[s])
            left = rows[s, at].reshape(256, W).astype(F32) - near
            rest[:, 32 * s : 32 * s + 32, :] = left.astype(BF16).reshape(8, 32, W)
        low = words[0, pl.ds(pl.multiple_of(to * 8, 8), 8), :]
        high = words[1, pl.ds(pl.multiple_of(to * 8, 8), 8), :]
        for k in range(8):
            pick = jnp.concatenate(
                [hot(w[k : k + 1] == sub128 + 1.0) for w in (low, high)], axis=1
            )
            sums = dot(pick, rest[k]).astype(BF16)
            table[0, pl.ds(to * 8 + k, 1)] = sums[0:64].reshape(1, 64, W)
            table[1, pl.ds(k * 8 + to, 1)] = sums[64:128].reshape(1, 64, W)

    def first_a(d, start):
        other, target = on_y(d)
        return remote(
            table.at[0, pl.ds(8 * other, 8)], table_1.at[0, y], ts.at[0, d], tr.at[0, d],
            target, start,
        )

    def first_b(d, at, size, start):
        other, target = on_z(d)
        return remote(
            table.at[1, pl.ds(8 * other + at, size)], table_1.at[1, z, pl.ds(at, size)],
            ts.at[1, d], tr.at[1, d], target, start,
        )

    def send_group(i, carry):
        far = lax.div(i + 1, 2)
        d = 4 + far - 2 * far * lax.rem(i, 2)
        to = lax.rem(y + d, NY)
        tabulate(to)
        first_a(d, True)
        for e in range(1, 8):
            first_b(e, to, 1, True)
        return carry

    lax.fori_loop(0, 7, send_group, 0)
    tabulate(y)
    for e in range(1, 8):
        first_b(e, y, 1, True)
    for h in range(2):
        table_1[h, pl.ds(here[h], 1)] = table[h, pl.ds(8 * here[h], 8)].reshape(1, 8, 64, W)
    wait(v_copies)
    for s in range(NL):
        coarse_out[:, W * s : W * s + W] = fresh_in[s]
    column[...] = columns(jnp.sum(count_in[...], axis=0)[0:1])
    for d in range(1, 8):
        first_a(d, False).wait()
        first_b(d, 0, 8, False).wait()

    def summed(h, j):
        total = jnp.zeros((64, W), F32)
        for i in range(8):
            total = total + table_1[h, i, pl.ds(j, 1)].reshape(64, W).astype(F32)
        return total.reshape(1, 64, W)

    def second(h, d, start):
        other, target = on[1 - h](d)
        return remote(
            part.at[h, other], part_2.at[h, here[1 - h]], ts.at[2 + h, d], tr.at[2 + h, d],
            target, start,
        )

    def send_sums(i, carry):
        far = lax.div(i + 1, 2)
        d = 4 + far - 2 * far * lax.rem(i, 2)
        for h in range(2):
            j = lax.rem(here[1 - h] + d, 8)
            part[h, pl.ds(j, 1)] = summed(h, j)
            second(h, d, True)
        return carry

    lax.fori_loop(0, 7, send_sums, 0)
    for h in range(2):
        part_2[h, pl.ds(here[1 - h], 1)] = summed(h, here[1 - h])
    for d in range(1, 8):
        for h in range(2):
            second(h, d, False).wait()
    for h in range(2):
        total = jnp.sum(part_2[h], axis=0)
        for q in range(4):
            last[2 * q + h] = total[16 * q : 16 * q + 16]
    e_copies = []
    for d in range(1, 8):
        other, target = member(d)
        e_copies.append(
            remote(last.at[other], last_in.at[m], es.at[2, d], er.at[2, d], target)
        )
    last_in[pl.ds(m, 1)] = last[pl.ds(m, 1)]
    mine[...] = column[pl.ds(pl.multiple_of(c * 64 + x * 16, 16), 16), :] + code_prior
    wait(e_copies)
    for s in range(NL):
        lanes = slice(W * s, W * s + W)
        codes_out[:, lanes] = (last_in[s] + code_prior * old_codes_ref[:, lanes]) / mine[...]


def body(frames, video_length, video_owner, video_cluster, frame_code, old_coarse, old_codes):
    dma = pltpu.SemaphoreType.DMA
    vmem = pl.BlockSpec(memory_space=pltpu.VMEM)
    hbm = pl.BlockSpec(memory_space=pl.ANY)
    return pl.pallas_call(
        kernel,
        out_shape=(
            jax.ShapeDtypeStruct((64, 1024), F32),
            jax.ShapeDtypeStruct((16, 1024), F32),
        ),
        in_specs=[hbm, vmem, vmem, vmem, vmem, hbm, vmem],
        out_specs=(vmem, vmem),
        scratch_shapes=[
            pltpu.VMEM((1024, 1024), BF16),
            pltpu.VMEM((16, 128), F32),
            pltpu.VMEM((NL, 1024, W), BF16),
            pltpu.VMEM((NL, 128, W), BF16),
            pltpu.VMEM((NL, 128, W), BF16),
            pltpu.VMEM((2, 256, W), BF16),
            pltpu.VMEM((40, 128), F32),
            pltpu.VMEM((NL, 40, 128), F32),
            pltpu.VMEM((1024, 2 * W), BF16),
            pltpu.VMEM((NL, 64, 32, W), BF16),
            pltpu.VMEM((NL, 64, 32, W), BF16),
            pltpu.VMEM((8, 256, W), BF16),
            pltpu.VMEM((2, 64, 128), F32),
            pltpu.VMEM((1024, 2048), BF16),
            pltpu.VMEM((NL, 128, W), BF16),
            pltpu.VMEM((128, 16, W), BF16),
            pltpu.VMEM((2, 8, 8, 16, W), BF16),
            pltpu.VMEM((2, 8, 8, 16, W), BF16),
            pltpu.VMEM((2, 8, 8, 16, W), BF16),
            pltpu.VMEM((2, 8, 8, 16, W), BF16),
            pltpu.VMEM((2, 8, 8, 16, W), BF16),
            pltpu.VMEM((2, 8, 16, 128), F32),
            pltpu.VMEM((2, 8, 16, 128), F32),
            pltpu.VMEM((2, 16, 128), F32),
            pltpu.VMEM((2, 8, 16, 128), F32),
            pltpu.VMEM((NL, 64, W), F32),
            pltpu.VMEM((NL, 64, W), F32),
            pltpu.VMEM((2, 64, 64, W), BF16),
            pltpu.VMEM((2, 8, 8, 64, W), BF16),
            pltpu.VMEM((2, 8, 64, W), F32),
            pltpu.VMEM((2, 8, 64, W), F32),
            pltpu.VMEM((NL, 16, W), F32),
            pltpu.VMEM((NL, 16, W), F32),
            pltpu.VMEM((8, 128), F32),
            pltpu.VMEM((NL, 8, 128), F32),
            pltpu.VMEM((128, 128), F32),
            dma((3,)),
            dma((8,)), dma((8,)),
            dma((8,)), dma((8,)),
            dma((8,)), dma((8,)),
            dma((4, 8)), dma((4, 8)),
            dma((4, 8)), dma((4, 8)),
            dma((4, 8)), dma((4, 8)),
            dma((4, 8)), dma((4, 8)),
            dma((3, 8)), dma((3, 8)),
        ],
        compiler_params=pltpu.CompilerParams(
            collective_id=0, has_side_effects=True, vmem_limit_bytes=56 << 20
        ),
    )(
        frames, video_length, video_owner, video_cluster,
        frame_code.reshape(8, 128), old_coarse, old_codes,
    )


def solution(mesh):
    placed = (
        P(("dp", "cent"), None),
        P(("dp", "cent"), None),
        P(("dp", "cent"), None),
        P(("dp", "cent"), None),
        P(("dp", "cent")),
        P("dp", None),
        P(("dp", "cent"), None),
    )
    return jax.shard_map(
        body,
        mesh=mesh,
        in_specs=placed,
        out_specs=(P(("dp", "cent"), None), P(("dp", "cent"), None)),
        check_vma=False,
    )
```

```python
import jax
import jax.numpy as jnp
from jax import lax
from jax.experimental import pallas as pl
from jax.experimental.pallas import tpu as pltpu
from jax.sharding import PartitionSpec as P

code_prior = 16.0
NL = 8
NY = 8
NZ = 8
W = 128
F32 = jnp.float32
BF16 = jnp.bfloat16


def iota(shape, dim):
    return lax.broadcasted_iota(jnp.int32, shape, dim).astype(F32)


def hot(condition):
    return jnp.where(condition, 1.0, 0.0).astype(BF16)


def columns(row):
    return jnp.transpose(jnp.broadcast_to(row, (128, 128)))


def dot(a, b):
    return jnp.dot(a, b, preferred_element_type=F32)


def dot_t(a, b):
    return lax.dot_general(a, b, (((1,), (1,)), ((), ())), preferred_element_type=F32)


def kernel(
    frames_ref, length_ref, owner_ref, cluster_ref, code_ref, old_ref, old_codes_ref,
    coarse_out, codes_out,
    frames_v, mine, theirs, pooled, pool_in, old_v,
    video, videos, into, out_of, amount, meta, metas, both, rows, picks, rest, words, wants, anchors,
    send_c, hop_c, got_c, back_0, back_1, back_2,
    note_0, note_1, note_s, note_2, fresh, fresh_in,
    table, table_1, part, part_2, last, last_in, count, count_in, column,
    load_sem, xs, xr, fs, fr, ps, pr, ns, nr, cs, cr, bs, br, ts, tr, es, er,
):
    dp = lax.axis_index("dp")
    x = lax.axis_index("cent")
    c = lax.rem(dp, 2)
    z = lax.rem(lax.div(dp, 2), NZ)
    y = lax.div(dp, 2 * NZ)
    m = x * 2 + c
    here = (y, z)

    def member(d):
        other = lax.rem(m + d, NL)
        return other, {"dp": (y * NZ + z) * 2 + lax.rem(other, 2), "cent": lax.div(other, 2)}

    def on_y(d):
        other = lax.rem(y + d, NY)
        return other, {"dp": (other * NZ + z) * 2 + c, "cent": x}

    def on_z(d):
        other = lax.rem(z + d, NZ)
        return other, {"dp": (y * NZ + other) * 2 + c, "cent": x}

    on = (on_y, on_z)

    def remote(src, dst, send, recv, target, start=True):
        copy = pltpu.make_async_remote_copy(
            src_ref=src, dst_ref=dst, send_sem=send, recv_sem=recv,
            device_id=target, device_id_type=pl.DeviceIdType.MESH,
        )
        if start:
            copy.start()
        return copy

    def local(src, dst, sem):
        copy = pltpu.make_async_copy(src, dst, sem)
        copy.start()
        return copy

    def wait(copies):
        for copy in copies:
            copy.wait()

    def spread(src, dst, send, recv, stage, axis):
        copies = []
        for d in range(1, 8):
            other, target = on[axis](d)
            copies.append(remote(src(other), dst, send.at[stage, d], recv.at[stage, d], target))
        return copies

    barrier = pltpu.get_barrier_semaphore()
    for d in range(1, 8):
        for find in (member, on_y, on_z):
            pl.semaphore_signal(
                barrier, inc=1, device_id=find(d)[1], device_id_type=pl.DeviceIdType.MESH
            )

    my_lanes = pl.ds(pl.multiple_of(m * W, W), W)
    load = local(frames_ref, frames_v, load_sem.at[0])
    load_mine = local(frames_ref.at[:, my_lanes], theirs.at[m], load_sem.at[1])
    load_old = local(old_ref.at[:, my_lanes], old_v.at[c], load_sem.at[2])

    sub128, lane128 = iota((128, 128), 0), iota((128, 128), 1)
    sub64 = iota((64, 128), 0)
    length = length_ref[...].astype(F32)
    through = hot(sub128 <= lane128)
    before = hot(sub128 < lane128)
    ends_row = dot(jnp.broadcast_to(length, (8, 128)).astype(BF16), through)[0:1]
    ends = columns(ends_row)
    lengths = columns(length)
    starts = ends - lengths
    pieces = []
    for a in range(8):
        position = lane128 + 128.0 * a
        pieces.append(hot(jnp.logical_and(position >= starts, position < ends)))
        meta[16 + a : 17 + a, :] = jnp.sum(
            jnp.where(ends <= position, 1.0, 0.0), axis=0, keepdims=True
        )
    of_video = jnp.concatenate(pieces, axis=1)

    owner_int = owner_ref[...]
    owner = owner_int.astype(F32)
    same = jnp.logical_and(columns(owner) == owner, sub128 < lane128)
    repeat = jnp.sum(jnp.where(same, 1.0, 0.0), axis=0, keepdims=True)
    half = jnp.bitwise_and(owner_int, 1)
    to_y = jnp.right_shift(owner_int, 4)
    to_z = jnp.bitwise_and(jnp.right_shift(owner_int, 1), NZ - 1)
    place = jnp.where(half == 0, to_y * NZ + to_z, to_z * NY + to_y)
    video[0:1, :] = (half * 1024 + place * 16).astype(F32) + repeat
    video[1:2, :] = cluster_ref[...].astype(F32) + 1.0
    video[2:3, :] = place.astype(F32)
    video[3:4, :] = repeat
    video[4:5, :] = half.astype(F32)
    video[5:8, :] = jnp.zeros((3, 128), F32)
    videos[pl.ds(m, 1)] = video[...].reshape(1, 8, 128)

    load.wait()
    for j in range(8):
        part_sum = dot(of_video, frames_v[:, 128 * j : 128 * j + 128])
        pooled[j] = (part_sum / lengths).astype(BF16)
    pl.semaphore_wait(barrier, 21)
    x_copies, f_copies, p_copies = [], [], []
    for d in range(1, 8):
        other, target = member(d)
        x_copies.append(remote(video, videos.at[m], xs.at[0, d], xr.at[0, d], target))
    for d in range(1, 8):
        other, target = member(d)
        p_copies.append(
            remote(pooled.at[other], pool_in.at[m], ps.at[d], pr.at[d], target)
        )
    partner = lax.rem(c + 1, 2)
    old_copy = remote(
        old_ref.at[:, pl.ds(pl.multiple_of((x * 2 + partner) * W, W), W)],
        old_v.at[c], xs.at[0, 0], xr.at[0, 0],
        {"dp": (y * NZ + z) * 2 + partner, "cent": x},
    )
    codes = code_ref[...]
    line_of = jnp.right_shift(codes, 7).astype(F32)
    in_line = jnp.bitwise_and(codes, 127).astype(F32)
    ones = jnp.ones((128, 128), BF16)
    seen = jnp.zeros((64, 128), F32)
    histogram = jnp.zeros((64, 128), F32)
    for a in range(8):
        match = hot(line_of[a : a + 1] == sub64)
        rank = jnp.sum(
            match.astype(F32) * (dot(match, before) + seen), axis=0, keepdims=True
        )
        meta[a : a + 1, :] = line_of[a : a + 1] * 32.0 + rank
        seen = seen + dot(match, ones)
        histogram = histogram + dot_t(match, hot(in_line[a : a + 1] == sub128))
    meta[8:16, :] = in_line
    metas[pl.ds(m, 1)] = meta[...].reshape(1, 24, 128)
    for j in range(8):
        note_0[0, j, 0:8, :] = histogram[8 * j : 8 * j + 8]
        note_0[1, j, 0:8, :] = jnp.zeros((8, 128), F32)

    m_copies = []
    for d in range(1, 8):
        other, target = member(d)
        m_copies.append(remote(meta, metas.at[m], xs.at[1, d], xr.at[1, d], target))
    for d in range(1, 8):
        other, target = member(d)
        lanes = pl.ds(pl.multiple_of(other * W, W), W)
        f_copies.append(
            remote(frames_ref.at[:, lanes], theirs.at[m], fs.at[d], fr.at[d], target)
        )
    pool_in[pl.ds(m, 1)] = pooled[pl.ds(m, 1)]

    wait(x_copies)
    places, values, halves, repeats = [
        [videos[s, i : i + 1, :] for s in range(NL)] for i in (2, 1, 4, 3)
    ]
    note = []
    for h in range(2):
        chosen = [
            jnp.where(
                jnp.logical_and(places[s] == sub64, halves[s] == float(h)), values[s], 0.0
            ).astype(BF16)
            for s in range(NL)
        ]
        lane = [hot(repeats[s] + (here[h] * 16 + 2 * s).astype(F32) == sub128) for s in range(NL)]
        note.append(dot_t(jnp.concatenate(chosen, axis=1), jnp.concatenate(lane, axis=1)))
    for h in range(2):
        for j in range(8):
            note_0[h, j, 8:16, :] = note[h][8 * j : 8 * j + 8]
    n_copies = []
    for h in range(2):
        n_copies += spread(lambda o: note_0.at[h, o], note_1.at[h, here[h]], ns, nr, h, h)
        note_1[h, pl.ds(here[h], 1)] = note_0[h, pl.ds(here[h], 1)]

    wait(p_copies)
    sub256, sub512 = iota((256, 128), 0), iota((512, 128), 0)

    def fill(chunk, carry):
        shift = (chunk * 512).astype(F32)
        pick = jnp.concatenate(
            [hot(videos[s, 0:1, :] + 2.0 * s - shift == sub512) for s in range(NL)], axis=1
        )
        filled = dot(pick, pool_in[...].reshape(1024, W))
        send_c[pl.ds(chunk * 32, 32)] = filled.astype(BF16).reshape(32, 16, W)
        return carry

    lax.fori_loop(0, 4, fill, 0)
    c_copies = []
    for h in range(2):
        c_copies += spread(
            lambda o: send_c.at[pl.ds(64 * h + 8 * o, 8)], hop_c.at[h, here[h]], cs, cr, h, h
        )
        hop_c[h, pl.ds(here[h], 1)] = send_c[pl.ds(64 * h + 8 * here[h], 8)].reshape(1, 8, 16, W)

    wait(n_copies)
    for h in range(2):
        note_s[h] = jnp.sum(note_1[h], axis=0)
    n_copies = []
    for h in range(2):
        n_copies += spread(
            lambda o: note_s.at[h], note_2.at[h, here[1 - h]], ns, nr, 2 + h, 1 - h
        )
        note_2[h, pl.ds(here[1 - h], 1)] = note_s[h].reshape(1, 16, 128)

    def take(d):
        s = lax.rem(m + NL - d, NL)
        for a in range(8):
            both[128 * a : 128 * a + 128, W:] = hot(
                columns(metas[s, 16 + a : 17 + a, :]) == lane128
            )
        both[:, :W] = theirs[s]

        def chunk_of(chunk, carry):
            shift = (chunk * 512).astype(F32)
            pick = jnp.concatenate(
                [hot(metas[s, a : a + 1, :] - shift == sub512) for a in range(8)], axis=1
            )
            out = dot(pick, both[...]).astype(BF16)
            rows[s, pl.ds(chunk * 16, 16)] = out[:, :W].reshape(16, 32, W)
            picks[s, pl.ds(chunk * 16, 16)] = out[:, W:].reshape(16, 32, W)
            return carry

        lax.fori_loop(0, 4, chunk_of, 0)

    def arrive(d):
        if d == 0:
            load_mine.wait()
        else:
            f_copies[d - 1].wait()
        take(d)

    def word(s, carry):
        offset = (lax.rem(s, 4) * 32).astype(F32)
        values, ranks = [], []
        for a in range(8):
            slot = metas[s, a : a + 1, :]
            line = jnp.floor(slot * (1.0 / 32.0))
            rank = slot - 32.0 * line + offset
            value = metas[s, 8 + a : 9 + a, :] + 1.0
            values.append(jnp.where(line == sub64, value, 0.0).astype(BF16))
            ranks.append(hot(rank == sub128))
        total = dot_t(jnp.concatenate(values, axis=1), jnp.concatenate(ranks, axis=1))
        group = pl.ds(lax.div(s, 4), 1)
        words[group] = words[group] + total.reshape(1, 64, 128)
        return carry

    def choose(s, carry):
        wanted = columns(videos[s, 0:1, :] + (2 * s).astype(F32))
        pick = [hot(wanted == lane128 + 128.0 * t) for t in range(16)]
        wants[pl.ds(pl.multiple_of(s * 128, 128), 128), :] = jnp.concatenate(pick, axis=1)
        return carry

    arrive(0)
    wait(m_copies)
    words[...] = jnp.zeros((2, 64, 128), F32)
    lax.fori_loop(0, NL, word, 0)
    lax.fori_loop(0, NL, choose, 0)

    wait(c_copies)
    c_copies = []
    for h in range(2):
        c_copies += spread(
            lambda o: hop_c.at[h, :, o], got_c.at[h, here[1 - h]], cs, cr, 2 + h, 1 - h
        )
        got_c[h, pl.ds(here[1 - h], 1)] = hop_c[h, :, pl.ds(here[1 - h], 1)].reshape(1, 8, 16, W)
    wait(n_copies)
    sub8, lane256 = iota((8, 128), 0), iota((128, 256), 1)
    for h in range(2):
        mask = sub8 == here[1 - h].astype(F32)
        ids = [
            jnp.sum(jnp.where(mask, note_2[h, j, 8:16, :], 0.0), axis=0, keepdims=True)
            for j in range(8)
        ]
        pick = jnp.concatenate([hot(ids[j] == sub256 + 1.0) for j in range(8)], axis=1)
        into[h] = pick
        amount[h] = dot(pick, jnp.ones((1024, W), BF16)) + 1.0
        for j in range(8):
            column_of = columns(ids[j])
            back = jnp.concatenate([column_of, column_of], axis=1) == lane256 + 1.0
            out_of[h, 128 * j : 128 * j + 128, :] = hot(back)
    counts = jnp.zeros((1, 128), F32)
    for j in range(8):
        counts = counts + jnp.sum(
            jnp.where(sub8 == z.astype(F32), note_2[0, j, 0:8, :], 0.0), axis=0, keepdims=True
        )
    count[...] = jnp.broadcast_to(counts, (8, 128))
    count_in[pl.ds(m, 1)] = count[...].reshape(1, 8, 128)
    arrive(1)
    arrive(2)
    load_old.wait()
    old_copy.wait()
    wait(c_copies)

    b_copies, v_copies, fresh_of = [], [], []
    for h in range(2):
        total = dot(into[h], got_c[h].reshape(1024, W))
        fresh_of.append((total + old_v[h].astype(F32)) / amount[h])
    for h in range(2):
        found = dot(out_of[h], fresh_of[h].astype(BF16)).astype(BF16)
        back_0[h] = found.reshape(8, 8, 16, W)
        b_copies += spread(
            lambda o: back_0.at[h, o], back_1.at[h, here[1 - h]], bs, br, h, 1 - h
        )
        back_1[h, pl.ds(here[1 - h], 1)] = back_0[h, pl.ds(here[1 - h], 1)]
    for h in range(2):
        for q in range(4):
            fresh[2 * q + h] = fresh_of[h][64 * q : 64 * q + 64]
    for d in range(1, 8):
        other, target = member(d)
        v_copies.append(
            remote(fresh.at[other], fresh_in.at[m], es.at[0, d], er.at[0, d], target)
        )
        v_copies.append(
            remote(count, count_in.at[m], es.at[1, d], er.at[1, d], target)
        )
    fresh_in[pl.ds(m, 1)] = fresh[pl.ds(m, 1)]
    arrive(3)
    arrive(4)
    arrive(5)

    wait(b_copies)
    b_copies = []
    for h in range(2):
        b_copies += spread(
            lambda o: back_1.at[h, :, o], back_2.at[h, here[h]], bs, br, 2 + h, h
        )
        back_2[h, pl.ds(here[h], 1)] = back_1[h, :, pl.ds(here[h], 1)].reshape(1, 8, 16, W)
    arrive(6)
    arrive(7)
    wait(b_copies)

    def read(chunk, carry):
        at = pl.multiple_of(chunk * 256, 256)
        found = dot(wants[pl.ds(at, 256), :], back_2[...].reshape(2048, W))
        anchors[pl.ds(chunk * 2, 2)] = found.astype(BF16).reshape(2, 128, W)
        return carry

    lax.fori_loop(0, 4, read, 0)

    def tabulate(to):
        at = pl.ds(to * 8, 8)
        for s in range(NL):
            near = dot(picks[s, at].reshape(256, W), anchors[s])
            left = rows[s, at].reshape(256, W).astype(F32) - near
            rest[:, 32 * s : 32 * s + 32, :] = left.astype(BF16).reshape(8, 32, W)
        low = words[0, pl.ds(pl.multiple_of(to * 8, 8), 8), :]
        high = words[1, pl.ds(pl.multiple_of(to * 8, 8), 8), :]
        for k in range(8):
            pick = jnp.concatenate(
                [hot(w[k : k + 1] == sub128 + 1.0) for w in (low, high)], axis=1
            )
            sums = dot(pick, rest[k]).astype(BF16)
            table[0, pl.ds(to * 8 + k, 1)] = sums[0:64].reshape(1, 64, W)
            table[1, pl.ds(k * 8 + to, 1)] = sums[64:128].reshape(1, 64, W)

    def first_a(d, start):
        other, target = on_y(d)
        return remote(
            table.at[0, pl.ds(8 * other, 8)], table_1.at[0, y], ts.at[0, d], tr.at[0, d],
            target, start,
        )

    def first_b(d, at, size, start):
        other, target = on_z(d)
        return remote(
            table.at[1, pl.ds(8 * other + at, size)], table_1.at[1, z, pl.ds(at, size)],
            ts.at[1, d], tr.at[1, d], target, start,
        )

    def send_group(i, carry):
        far = lax.div(i + 1, 2)
        d = 4 + far - 2 * far * lax.rem(i, 2)
        to = lax.rem(y + d, NY)
        tabulate(to)
        first_a(d, True)
        for e in range(1, 8):
            first_b(e, to, 1, True)
        return carry

    lax.fori_loop(0, 7, send_group, 0)
    tabulate(y)
    for e in range(1, 8):
        first_b(e, y, 1, True)
    for h in range(2):
        table_1[h, pl.ds(here[h], 1)] = table[h, pl.ds(8 * here[h], 8)].reshape(1, 8, 64, W)
    wait(v_copies)
    for s in range(NL):
        coarse_out[:, W * s : W * s + W] = fresh_in[s]
    column[...] = columns(jnp.sum(count_in[...], axis=0)[0:1])
    for d in range(1, 8):
        first_a(d, False).wait()
        first_b(d, 0, 8, False).wait()

    def summed(h, j):
        total = jnp.zeros((64, W), F32)
        for i in range(8):
            total = total + table_1[h, i, pl.ds(j, 1)].reshape(64, W).astype(F32)
        return total.reshape(1, 64, W)

    def second(h, d, start):
        other, target = on[1 - h](d)
        return remote(
            part.at[h, other], part_2.at[h, here[1 - h]], ts.at[2 + h, d], tr.at[2 + h, d],
            target, start,
        )

    def send_sums(i, carry):
        far = lax.div(i + 1, 2)
        d = 4 + far - 2 * far * lax.rem(i, 2)
        for h in range(2):
            j = lax.rem(here[1 - h] + d, 8)
            part[h, pl.ds(j, 1)] = summed(h, j)
            second(h, d, True)
        return carry

    lax.fori_loop(0, 7, send_sums, 0)
    for h in range(2):
        part_2[h, pl.ds(here[1 - h], 1)] = summed(h, here[1 - h])
    for d in range(1, 8):
        for h in range(2):
            second(h, d, False).wait()
    for h in range(2):
        total = jnp.sum(part_2[h], axis=0)
        for q in range(4):
            last[2 * q + h] = total[16 * q : 16 * q + 16]
    e_copies = []
    for d in range(1, 8):
        other, target = member(d)
        e_copies.append(
            remote(last.at[other], last_in.at[m], es.at[2, d], er.at[2, d], target)
        )
    last_in[pl.ds(m, 1)] = last[pl.ds(m, 1)]
    mine[...] = column[pl.ds(pl.multiple_of(c * 64 + x * 16, 16), 16), :] + code_prior
    wait(e_copies)
    for s in range(NL):
        lanes = slice(W * s, W * s + W)
        codes_out[:, lanes] = (last_in[s] + code_prior * old_codes_ref[:, lanes]) / mine[...]


def hand_on(coarse_in, codes_in, coarse_out, codes_out):
    coarse_out[...] = coarse_in[...]
    codes_out[...] = codes_in[...]


def body(frames, video_length, video_owner, video_cluster, frame_code, old_coarse, old_codes):
    dma = pltpu.SemaphoreType.DMA
    vmem = pl.BlockSpec(memory_space=pltpu.VMEM)
    hbm = pl.BlockSpec(memory_space=pl.ANY)
    coarse, codes = pl.pallas_call(
        kernel,
        out_shape=(
            jax.ShapeDtypeStruct((64, 1024), F32),
            jax.ShapeDtypeStruct((16, 1024), F32),
        ),
        in_specs=[hbm, vmem, vmem, vmem, vmem, hbm, vmem],
        out_specs=(vmem, vmem),
        scratch_shapes=[
            pltpu.VMEM((1024, 1024), BF16),
            pltpu.VMEM((16, 128), F32),
            pltpu.VMEM((NL, 1024, W), BF16),
            pltpu.VMEM((NL, 128, W), BF16),
            pltpu.VMEM((NL, 128, W), BF16),
            pltpu.VMEM((2, 256, W), BF16),
            pltpu.VMEM((8, 128), F32),
            pltpu.VMEM((NL, 8, 128), F32),
            pltpu.VMEM((2, 256, 1024), BF16),
            pltpu.VMEM((2, 1024, 256), BF16),
            pltpu.VMEM((2, 256, W), F32),
            pltpu.VMEM((24, 128), F32),
            pltpu.VMEM((NL, 24, 128), F32),
            pltpu.VMEM((1024, 2 * W), BF16),
            pltpu.VMEM((NL, 64, 32, W), BF16),
            pltpu.VMEM((NL, 64, 32, W), BF16),
            pltpu.VMEM((8, 256, W), BF16),
            pltpu.VMEM((2, 64, 128), F32),
            pltpu.VMEM((1024, 2048), BF16),
            pltpu.VMEM((NL, 128, W), BF16),
            pltpu.VMEM((128, 16, W), BF16),
            pltpu.VMEM((2, 8, 8, 16, W), BF16),
            pltpu.VMEM((2, 8, 8, 16, W), BF16),
            pltpu.VMEM((2, 8, 8, 16, W), BF16),
            pltpu.VMEM((2, 8, 8, 16, W), BF16),
            pltpu.VMEM((2, 8, 8, 16, W), BF16),
            pltpu.VMEM((2, 8, 16, 128), F32),
            pltpu.VMEM((2, 8, 16, 128), F32),
            pltpu.VMEM((2, 16, 128), F32),
            pltpu.VMEM((2, 8, 16, 128), F32),
            pltpu.VMEM((NL, 64, W), F32),
            pltpu.VMEM((NL, 64, W), F32),
            pltpu.VMEM((2, 64, 64, W), BF16),
            pltpu.VMEM((2, 8, 8, 64, W), BF16),
            pltpu.VMEM((2, 8, 64, W), F32),
            pltpu.VMEM((2, 8, 64, W), F32),
            pltpu.VMEM((NL, 16, W), F32),
            pltpu.VMEM((NL, 16, W), F32),
            pltpu.VMEM((8, 128), F32),
            pltpu.VMEM((NL, 8, 128), F32),
            pltpu.VMEM((128, 128), F32),
            dma((3,)),
            dma((2, 8)), dma((2, 8)),
            dma((8,)), dma((8,)),
            dma((8,)), dma((8,)),
            dma((4, 8)), dma((4, 8)),
            dma((4, 8)), dma((4, 8)),
            dma((4, 8)), dma((4, 8)),
            dma((4, 8)), dma((4, 8)),
            dma((3, 8)), dma((3, 8)),
        ],
        compiler_params=pltpu.CompilerParams(
            collective_id=0, has_side_effects=True, vmem_limit_bytes=56 << 20
        ),
    )(
        frames, video_length, video_owner, video_cluster,
        frame_code.reshape(8, 128), old_coarse, old_codes,
    )
    return pl.pallas_call(
        hand_on,
        out_shape=(
            jax.ShapeDtypeStruct((64, 1024), F32),
            jax.ShapeDtypeStruct((16, 1024), F32),
        ),
        in_specs=[vmem, vmem],
        out_specs=(vmem, vmem),
    )(coarse, codes)


def solution(mesh):
    placed = (
        P(("dp", "cent"), None),
        P(("dp", "cent"), None),
        P(("dp", "cent"), None),
        P(("dp", "cent"), None),
        P(("dp", "cent")),
        P("dp", None),
        P(("dp", "cent"), None),
    )
    return jax.shard_map(
        body,
        mesh=mesh,
        in_specs=placed,
        out_specs=(P(("dp", "cent"), None), P(("dp", "cent"), None)),
        check_vma=False,
    )
```

```python
import jax
import jax.numpy as jnp
from jax import lax
from jax.experimental import pallas as pl
from jax.experimental.pallas import tpu as pltpu
from jax.sharding import PartitionSpec as P

code_prior = 16.0
NL = 8
NY = 8
NZ = 8
W = 128
F32 = jnp.float32
BF16 = jnp.bfloat16


def iota(shape, dim):
    return lax.broadcasted_iota(jnp.int32, shape, dim).astype(F32)


def hot(condition):
    return jnp.where(condition, 1.0, 0.0).astype(BF16)


def columns(row):
    return jnp.transpose(jnp.broadcast_to(row, (128, 128)))


def dot(a, b):
    return jnp.dot(a, b, preferred_element_type=F32)


def dot_t(a, b):
    return lax.dot_general(a, b, (((1,), (1,)), ((), ())), preferred_element_type=F32)


def kernel(
    frames_ref, length_ref, owner_ref, cluster_ref, code_ref, old_ref, old_codes_ref,
    coarse_out, codes_out,
    frames_v, mine, theirs, pooled, pool_in, old_v,
    video, videos, into, out_of, amount, meta, metas, both, rows, picks, rest, words, wants, wide, anchors,
    send_c, hop_c, got_c, back_0, back_1, back_2,
    note_0, note_1, note_s, note_2, fresh, fresh_in,
    table, table_1, part, part_2, last, last_in, count, count_in, column,
    load_sem, xs, xr, fs, fr, ps, pr, ns, nr, cs, cr, bs, br, ts, tr, es, er,
):
    dp = lax.axis_index("dp")
    x = lax.axis_index("cent")
    c = lax.rem(dp, 2)
    z = lax.rem(lax.div(dp, 2), NZ)
    y = lax.div(dp, 2 * NZ)
    m = x * 2 + c
    here = (y, z)

    def member(d):
        other = lax.rem(m + d, NL)
        return other, {"dp": (y * NZ + z) * 2 + lax.rem(other, 2), "cent": lax.div(other, 2)}

    def on_y(d):
        other = lax.rem(y + d, NY)
        return other, {"dp": (other * NZ + z) * 2 + c, "cent": x}

    def on_z(d):
        other = lax.rem(z + d, NZ)
        return other, {"dp": (y * NZ + other) * 2 + c, "cent": x}

    on = (on_y, on_z)

    def remote(src, dst, send, recv, target, start=True):
        copy = pltpu.make_async_remote_copy(
            src_ref=src, dst_ref=dst, send_sem=send, recv_sem=recv,
            device_id=target, device_id_type=pl.DeviceIdType.MESH,
        )
        if start:
            copy.start()
        return copy

    def local(src, dst, sem):
        copy = pltpu.make_async_copy(src, dst, sem)
        copy.start()
        return copy

    def wait(copies):
        for copy in copies:
            copy.wait()

    def spread(src, dst, send, recv, stage, axis):
        copies = []
        for d in range(1, 8):
            other, target = on[axis](d)
            copies.append(remote(src(other), dst, send.at[stage, d], recv.at[stage, d], target))
        return copies

    barrier = pltpu.get_barrier_semaphore()
    for d in range(1, 8):
        for find in (member, on_y, on_z):
            pl.semaphore_signal(
                barrier, inc=1, device_id=find(d)[1], device_id_type=pl.DeviceIdType.MESH
            )

    my_lanes = pl.ds(pl.multiple_of(m * W, W), W)
    loads = []
    for d in range(1, 8):
        lanes = pl.ds(pl.multiple_of(member(d)[0] * W, W), W)
        loads.append(local(frames_ref.at[:, lanes], frames_v.at[d], load_sem.at[d]))
    load_mine = local(frames_ref.at[:, my_lanes], theirs.at[m], load_sem.at[0])
    load_old = local(old_ref.at[:, my_lanes], old_v.at[c], load_sem.at[8])

    sub128, lane128 = iota((128, 128), 0), iota((128, 128), 1)
    sub64 = iota((64, 128), 0)
    length = length_ref[...].astype(F32)
    through = hot(sub128 <= lane128)
    before = hot(sub128 < lane128)
    ends_row = dot(jnp.broadcast_to(length, (8, 128)).astype(BF16), through)[0:1]
    ends = columns(ends_row)
    lengths = columns(length)
    starts = ends - lengths
    pieces = []
    for a in range(8):
        position = lane128 + 128.0 * a
        pieces.append(hot(jnp.logical_and(position >= starts, position < ends)))
        meta[16 + a : 17 + a, :] = jnp.sum(
            jnp.where(ends <= position, 1.0, 0.0), axis=0, keepdims=True
        )
    of_video = jnp.concatenate(pieces, axis=1)

    owner_int = owner_ref[...]
    owner = owner_int.astype(F32)
    same = jnp.logical_and(columns(owner) == owner, sub128 < lane128)
    repeat = jnp.sum(jnp.where(same, 1.0, 0.0), axis=0, keepdims=True)
    half = jnp.bitwise_and(owner_int, 1)
    to_y = jnp.right_shift(owner_int, 4)
    to_z = jnp.bitwise_and(jnp.right_shift(owner_int, 1), NZ - 1)
    place = jnp.where(half == 0, to_y * NZ + to_z, to_z * NY + to_y)
    video[0:1, :] = (half * 1024 + place * 16).astype(F32) + repeat
    video[1:2, :] = cluster_ref[...].astype(F32) + 1.0
    video[2:3, :] = place.astype(F32)
    video[3:4, :] = repeat
    video[4:5, :] = half.astype(F32)
    video[5:8, :] = jnp.zeros((3, 128), F32)
    videos[pl.ds(m, 1)] = video[...].reshape(1, 8, 128)

    pl.semaphore_wait(barrier, 21)
    x_copies, f_copies, p_copies = [], [], []
    for d in range(1, 8):
        other, target = member(d)
        x_copies.append(remote(video, videos.at[m], xs.at[0, d], xr.at[0, d], target))
    for d in range(1, 8):
        other, target = member(d)
        loads[d - 1].wait()
        pooled[d] = (dot(of_video, frames_v[d]) / lengths).astype(BF16)
        p_copies.append(
            remote(pooled.at[d], pool_in.at[m], ps.at[d], pr.at[d], target)
        )
    partner = lax.rem(c + 1, 2)
    old_copy = remote(
        old_ref.at[:, pl.ds(pl.multiple_of((x * 2 + partner) * W, W), W)],
        old_v.at[c], xs.at[0, 0], xr.at[0, 0],
        {"dp": (y * NZ + z) * 2 + partner, "cent": x},
    )
    codes = code_ref[...]
    line_of = jnp.right_shift(codes, 7).astype(F32)
    in_line = jnp.bitwise_and(codes, 127).astype(F32)
    ones = jnp.ones((128, 128), BF16)
    seen = jnp.zeros((64, 128), F32)
    histogram = jnp.zeros((64, 128), F32)
    for a in range(8):
        match = hot(line_of[a : a + 1] == sub64)
        rank = jnp.sum(
            match.astype(F32) * (dot(match, before) + seen), axis=0, keepdims=True
        )
        meta[a : a + 1, :] = line_of[a : a + 1] * 32.0 + rank
        seen = seen + dot(match, ones)
        histogram = histogram + dot_t(match, hot(in_line[a : a + 1] == sub128))
    meta[8:16, :] = in_line
    metas[pl.ds(m, 1)] = meta[...].reshape(1, 24, 128)
    for j in range(8):
        note_0[0, j, 0:8, :] = histogram[8 * j : 8 * j + 8]
        note_0[1, j, 0:8, :] = jnp.zeros((8, 128), F32)

    m_copies = []
    for d in range(1, 8):
        other, target = member(d)
        m_copies.append(remote(meta, metas.at[m], xs.at[1, d], xr.at[1, d], target))
    for d in range(1, 8):
        other, target = member(d)
        f_copies.append(
            remote(frames_v.at[d], theirs.at[m], fs.at[d], fr.at[d], target)
        )
    load_mine.wait()
    own = dot(of_video, theirs[pl.ds(m, 1)].reshape(1024, W)) / lengths
    pool_in[pl.ds(m, 1)] = own.astype(BF16).reshape(1, 128, W)

    wait(x_copies)
    places, values, halves, repeats = [
        [videos[s, i : i + 1, :] for s in range(NL)] for i in (2, 1, 4, 3)
    ]
    note = []
    for h in range(2):
        chosen = [
            jnp.where(
                jnp.logical_and(places[s] == sub64, halves[s] == float(h)), values[s], 0.0
            ).astype(BF16)
            for s in range(NL)
        ]
        lane = [hot(repeats[s] + (here[h] * 16 + 2 * s).astype(F32) == sub128) for s in range(NL)]
        note.append(dot_t(jnp.concatenate(chosen, axis=1), jnp.concatenate(lane, axis=1)))
    for h in range(2):
        for j in range(8):
            note_0[h, j, 8:16, :] = note[h][8 * j : 8 * j + 8]
    n_copies = []
    for h in range(2):
        n_copies += spread(lambda o: note_0.at[h, o], note_1.at[h, here[h]], ns, nr, h, h)
        note_1[h, pl.ds(here[h], 1)] = note_0[h, pl.ds(here[h], 1)]

    wait(p_copies)
    sub256, sub512 = iota((256, 128), 0), iota((512, 128), 0)

    def fill(chunk, carry):
        shift = (chunk * 512).astype(F32)
        pick = jnp.concatenate(
            [hot(videos[s, 0:1, :] + 2.0 * s - shift == sub512) for s in range(NL)], axis=1
        )
        filled = dot(pick, pool_in[...].reshape(1024, W))
        send_c[pl.ds(chunk * 32, 32)] = filled.astype(BF16).reshape(32, 16, W)
        return carry

    lax.fori_loop(0, 4, fill, 0)
    c_copies = []
    for h in range(2):
        c_copies += spread(
            lambda o: send_c.at[pl.ds(64 * h + 8 * o, 8)], hop_c.at[h, here[h]], cs, cr, h, h
        )
        hop_c[h, pl.ds(here[h], 1)] = send_c[pl.ds(64 * h + 8 * here[h], 8)].reshape(1, 8, 16, W)

    wait(n_copies)
    for h in range(2):
        note_s[h] = jnp.sum(note_1[h], axis=0)
    n_copies = []
    for h in range(2):
        n_copies += spread(
            lambda o: note_s.at[h], note_2.at[h, here[1 - h]], ns, nr, 2 + h, 1 - h
        )
        note_2[h, pl.ds(here[1 - h], 1)] = note_s[h].reshape(1, 16, 128)

    def take(d):
        s = lax.rem(m + NL - d, NL)
        for a in range(8):
            both[128 * a : 128 * a + 128, W:] = hot(
                columns(metas[s, 16 + a : 17 + a, :]) == lane128
            )
        both[:, :W] = theirs[s]

        def chunk_of(chunk, carry):
            shift = (chunk * 512).astype(F32)
            pick = jnp.concatenate(
                [hot(metas[s, a : a + 1, :] - shift == sub512) for a in range(8)], axis=1
            )
            out = dot(pick, both[...]).astype(BF16)
            rows[s, pl.ds(chunk * 16, 16)] = out[:, :W].reshape(16, 32, W)
            picks[s, pl.ds(chunk * 16, 16)] = out[:, W:].reshape(16, 32, W)
            return carry

        lax.fori_loop(0, 4, chunk_of, 0)

    def arrive(d):
        if d > 0:
            f_copies[d - 1].wait()
        take(d)

    def word(s, carry):
        offset = (lax.rem(s, 4) * 32).astype(F32)
        values, ranks = [], []
        for a in range(8):
            slot = metas[s, a : a + 1, :]
            line = jnp.floor(slot * (1.0 / 32.0))
            rank = slot - 32.0 * line + offset
            value = metas[s, 8 + a : 9 + a, :] + 1.0
            values.append(jnp.where(line == sub64, value, 0.0).astype(BF16))
            ranks.append(hot(rank == sub128))
        total = dot_t(jnp.concatenate(values, axis=1), jnp.concatenate(ranks, axis=1))
        group = pl.ds(lax.div(s, 4), 1)
        words[group] = words[group] + total.reshape(1, 64, 128)
        return carry

    def choose(s, carry):
        info = videos[s]
        wanted = columns(info[3:4] * 128.0 + info[4:5] * 64.0 + info[2:3])
        pick = [hot(wanted == lane128 + 128.0 * t) for t in range(2)]
        wants[pl.ds(s, 1)] = jnp.concatenate(pick, axis=1).reshape(1, 128, 256)
        return carry

    arrive(0)
    wait(m_copies)
    words[...] = jnp.zeros((2, 64, 128), F32)
    lax.fori_loop(0, NL, word, 0)
    lax.fori_loop(0, NL, choose, 0)

    wait(c_copies)
    c_copies = []
    for h in range(2):
        c_copies += spread(
            lambda o: hop_c.at[h, :, o], got_c.at[h, here[1 - h]], cs, cr, 2 + h, 1 - h
        )
        got_c[h, pl.ds(here[1 - h], 1)] = hop_c[h, :, pl.ds(here[1 - h], 1)].reshape(1, 8, 16, W)
    wait(n_copies)
    sub8, lane256 = iota((8, 128), 0), iota((128, 256), 1)
    for h in range(2):
        mask = sub8 == here[1 - h].astype(F32)
        ids = [
            jnp.sum(jnp.where(mask, note_2[h, j, 8:16, :], 0.0), axis=0, keepdims=True)
            for j in range(8)
        ]
        pick = jnp.concatenate([hot(ids[j] == sub256 + 1.0) for j in range(8)], axis=1)
        into[h] = pick
        amount[h] = dot(pick, jnp.ones((1024, W), BF16)) + 1.0
        for j in range(8):
            column_of = columns(ids[j])
            back = jnp.concatenate([column_of, column_of], axis=1) == lane256 + 1.0
            out_of[h, 128 * j : 128 * j + 128, :] = hot(back)
    counts = jnp.zeros((1, 128), F32)
    for j in range(8):
        counts = counts + jnp.sum(
            jnp.where(sub8 == z.astype(F32), note_2[0, j, 0:8, :], 0.0), axis=0, keepdims=True
        )
    count[...] = jnp.broadcast_to(counts, (8, 128))
    count_in[pl.ds(m, 1)] = count[...].reshape(1, 8, 128)
    arrive(1)
    load_old.wait()
    old_copy.wait()
    wait(c_copies)

    b_copies, v_copies, fresh_of = [], [], []
    for h in range(2):
        total = dot(into[h], got_c[h].reshape(1024, W))
        fresh_of.append((total + old_v[h].astype(F32)) / amount[h])
    for h in range(2):
        found = dot(out_of[h], fresh_of[h].astype(BF16)).astype(BF16)
        back_0[h] = found.reshape(8, 8, 16, W)
        b_copies += spread(
            lambda o: back_0.at[h, o], back_1.at[h, here[1 - h]], bs, br, h, 1 - h
        )
        back_1[h, pl.ds(here[1 - h], 1)] = back_0[h, pl.ds(here[1 - h], 1)]
    for h in range(2):
        for q in range(4):
            fresh[2 * q + h] = fresh_of[h][64 * q : 64 * q + 64]
    for d in range(1, 8):
        other, target = member(d)
        v_copies.append(
            remote(fresh.at[other], fresh_in.at[m], es.at[0, d], er.at[0, d], target)
        )
        v_copies.append(
            remote(count, count_in.at[m], es.at[1, d], er.at[1, d], target)
        )
    fresh_in[pl.ds(m, 1)] = fresh[pl.ds(m, 1)]
    arrive(2)
    arrive(3)
    arrive(4)

    wait(b_copies)
    b_copies = []
    for h in range(2):
        b_copies += spread(
            lambda o: back_1.at[h, :, o], back_2.at[h, here[h]], bs, br, 2 + h, h
        )
        back_2[h, pl.ds(here[h], 1)] = back_1[h, :, pl.ds(here[h], 1)].reshape(1, 8, 16, W)
    arrive(5)
    arrive(6)
    arrive(7)
    wait(b_copies)

    wide[...] = back_2[...].reshape(2048, W).astype(F32)
    for s in range(NL):
        found = [wide[pl.ds(2 * s + r, 128, stride=16), :].astype(BF16) for r in range(2)]
        anchors[s] = dot(wants[s], jnp.concatenate(found, axis=0)).astype(BF16)

    def tabulate(to):
        at = pl.ds(to * 8, 8)
        for s in range(NL):
            near = dot(picks[s, at].reshape(256, W), anchors[s])
            left = rows[s, at].reshape(256, W).astype(F32) - near
            rest[:, 32 * s : 32 * s + 32, :] = left.astype(BF16).reshape(8, 32, W)
        low = words[0, pl.ds(pl.multiple_of(to * 8, 8), 8), :]
        high = words[1, pl.ds(pl.multiple_of(to * 8, 8), 8), :]
        for k in range(8):
            pick = jnp.concatenate(
                [hot(w[k : k + 1] == sub128 + 1.0) for w in (low, high)], axis=1
            )
            sums = dot(pick, rest[k]).astype(BF16)
            table[0, pl.ds(to * 8 + k, 1)] = sums[0:64].reshape(1, 64, W)
            table[1, pl.ds(k * 8 + to, 1)] = sums[64:128].reshape(1, 64, W)

    def first_a(d, start):
        other, target = on_y(d)
        return remote(
            table.at[0, pl.ds(8 * other, 8)], table_1.at[0, y], ts.at[0, d], tr.at[0, d],
            target, start,
        )

    def first_b(d, at, size, start):
        other, target = on_z(d)
        return remote(
            table.at[1, pl.ds(8 * other + at, size)], table_1.at[1, z, pl.ds(at, size)],
            ts.at[1, d], tr.at[1, d], target, start,
        )

    def send_group(i, carry):
        far = lax.div(i + 1, 2)
        d = 4 + far - 2 * far * lax.rem(i, 2)
        to = lax.rem(y + d, NY)
        tabulate(to)
        first_a(d, True)
        for e in range(1, 8):
            first_b(e, to, 1, True)
        return carry

    lax.fori_loop(0, 7, send_group, 0)
    tabulate(y)
    for e in range(1, 8):
        first_b(e, y, 1, True)
    for h in range(2):
        table_1[h, pl.ds(here[h], 1)] = table[h, pl.ds(8 * here[h], 8)].reshape(1, 8, 64, W)
    wait(v_copies)
    for s in range(NL):
        coarse_out[:, W * s : W * s + W] = fresh_in[s]
    column[...] = columns(jnp.sum(count_in[...], axis=0)[0:1])
    for d in range(1, 8):
        first_a(d, False).wait()
        first_b(d, 0, 8, False).wait()

    def summed(h, j):
        total = jnp.zeros((64, W), F32)
        for i in range(8):
            total = total + table_1[h, i, pl.ds(j, 1)].reshape(64, W).astype(F32)
        return total.reshape(1, 64, W)

    def second(h, d, start):
        other, target = on[1 - h](d)
        return remote(
            part.at[h, other], part_2.at[h, here[1 - h]], ts.at[2 + h, d], tr.at[2 + h, d],
            target, start,
        )

    def send_sums(i, carry):
        far = lax.div(i + 1, 2)
        d = 4 + far - 2 * far * lax.rem(i, 2)
        for h in range(2):
            j = lax.rem(here[1 - h] + d, 8)
            part[h, pl.ds(j, 1)] = summed(h, j)
            second(h, d, True)
        return carry

    lax.fori_loop(0, 7, send_sums, 0)
    for h in range(2):
        part_2[h, pl.ds(here[1 - h], 1)] = summed(h, here[1 - h])
    for d in range(1, 8):
        for h in range(2):
            second(h, d, False).wait()
    for h in range(2):
        total = jnp.sum(part_2[h], axis=0)
        for q in range(4):
            last[2 * q + h] = total[16 * q : 16 * q + 16]
    e_copies = []
    for d in range(1, 8):
        other, target = member(d)
        e_copies.append(
            remote(last.at[other], last_in.at[m], es.at[2, d], er.at[2, d], target)
        )
    last_in[pl.ds(m, 1)] = last[pl.ds(m, 1)]
    mine[...] = column[pl.ds(pl.multiple_of(c * 64 + x * 16, 16), 16), :] + code_prior
    wait(e_copies)
    for s in range(NL):
        lanes = slice(W * s, W * s + W)
        codes_out[:, lanes] = (last_in[s] + code_prior * old_codes_ref[:, lanes]) / mine[...]


def hand_on(coarse_in, codes_in, coarse_out, codes_out):
    coarse_out[...] = coarse_in[...]
    codes_out[...] = codes_in[...]


def body(frames, video_length, video_owner, video_cluster, frame_code, old_coarse, old_codes):
    dma = pltpu.SemaphoreType.DMA
    vmem = pl.BlockSpec(memory_space=pltpu.VMEM)
    hbm = pl.BlockSpec(memory_space=pl.ANY)
    coarse, codes = pl.pallas_call(
        kernel,
        out_shape=(
            jax.ShapeDtypeStruct((64, 1024), F32),
            jax.ShapeDtypeStruct((16, 1024), F32),
        ),
        in_specs=[hbm, vmem, vmem, vmem, vmem, hbm, vmem],
        out_specs=(vmem, vmem),
        scratch_shapes=[
            pltpu.VMEM((NL, 1024, W), BF16),
            pltpu.VMEM((16, 128), F32),
            pltpu.VMEM((NL, 1024, W), BF16),
            pltpu.VMEM((NL, 128, W), BF16),
            pltpu.VMEM((NL, 128, W), BF16),
            pltpu.VMEM((2, 256, W), BF16),
            pltpu.VMEM((8, 128), F32),
            pltpu.VMEM((NL, 8, 128), F32),
            pltpu.VMEM((2, 256, 1024), BF16),
            pltpu.VMEM((2, 1024, 256), BF16),
            pltpu.VMEM((2, 256, W), F32),
            pltpu.VMEM((24, 128), F32),
            pltpu.VMEM((NL, 24, 128), F32),
            pltpu.VMEM((1024, 2 * W), BF16),
            pltpu.VMEM((NL, 64, 32, W), BF16),
            pltpu.VMEM((NL, 64, 32, W), BF16),
            pltpu.VMEM((8, 256, W), BF16),
            pltpu.VMEM((2, 64, 128), F32),
            pltpu.VMEM((NL, 128, 256), BF16),
            pltpu.VMEM((2048, W), F32),
            pltpu.VMEM((NL, 128, W), BF16),
            pltpu.VMEM((128, 16, W), BF16),
            pltpu.VMEM((2, 8, 8, 16, W), BF16),
            pltpu.VMEM((2, 8, 8, 16, W), BF16),
            pltpu.VMEM((2, 8, 8, 16, W), BF16),
            pltpu.VMEM((2, 8, 8, 16, W), BF16),
            pltpu.VMEM((2, 8, 8, 16, W), BF16),
            pltpu.VMEM((2, 8, 16, 128), F32),
            pltpu.VMEM((2, 8, 16, 128), F32),
            pltpu.VMEM((2, 16, 128), F32),
            pltpu.VMEM((2, 8, 16, 128), F32),
            pltpu.VMEM((NL, 64, W), F32),
            pltpu.VMEM((NL, 64, W), F32),
            pltpu.VMEM((2, 64, 64, W), BF16),
            pltpu.VMEM((2, 8, 8, 64, W), BF16),
            pltpu.VMEM((2, 8, 64, W), F32),
            pltpu.VMEM((2, 8, 64, W), F32),
            pltpu.VMEM((NL, 16, W), F32),
            pltpu.VMEM((NL, 16, W), F32),
            pltpu.VMEM((8, 128), F32),
            pltpu.VMEM((NL, 8, 128), F32),
            pltpu.VMEM((128, 128), F32),
            dma((9,)),
            dma((2, 8)), dma((2, 8)),
            dma((8,)), dma((8,)),
            dma((8,)), dma((8,)),
            dma((4, 8)), dma((4, 8)),
            dma((4, 8)), dma((4, 8)),
            dma((4, 8)), dma((4, 8)),
            dma((4, 8)), dma((4, 8)),
            dma((3, 8)), dma((3, 8)),
        ],
        compiler_params=pltpu.CompilerParams(
            collective_id=0, has_side_effects=True, vmem_limit_bytes=56 << 20
        ),
    )(
        frames, video_length, video_owner, video_cluster,
        frame_code.reshape(8, 128), old_coarse, old_codes,
    )
    return pl.pallas_call(
        hand_on,
        out_shape=(
            jax.ShapeDtypeStruct((64, 1024), F32),
            jax.ShapeDtypeStruct((16, 1024), F32),
        ),
        in_specs=[vmem, vmem],
        out_specs=(vmem, vmem),
    )(coarse, codes)


def solution(mesh):
    placed = (
        P(("dp", "cent"), None),
        P(("dp", "cent"), None),
        P(("dp", "cent"), None),
        P(("dp", "cent"), None),
        P(("dp", "cent")),
        P("dp", None),
        P(("dp", "cent"), None),
    )
    return jax.shard_map(
        body,
        mesh=mesh,
        in_specs=placed,
        out_specs=(P(("dp", "cent"), None), P(("dp", "cent"), None)),
        check_vma=False,
    )
```

```python
import jax
import jax.numpy as jnp
from jax import lax
from jax.experimental import pallas as pl
from jax.experimental.pallas import tpu as pltpu
from jax.sharding import PartitionSpec as P

code_prior = 16.0
NL = 8
NY = 8
NZ = 8
W = 128
FAR = (4, 3, 5, 2, 6, 1, 7)
F32 = jnp.float32
BF16 = jnp.bfloat16


def iota(shape, dim):
    return lax.broadcasted_iota(jnp.int32, shape, dim).astype(F32)


def hot(condition):
    return jnp.where(condition, 1.0, 0.0).astype(BF16)


def columns(row):
    return jnp.transpose(jnp.broadcast_to(row, (128, 128)))


def dot(a, b):
    return jnp.dot(a, b, preferred_element_type=F32)


def dot_t(a, b):
    return lax.dot_general(a, b, (((1,), (1,)), ((), ())), preferred_element_type=F32)


def kernel(
    frames_ref, length_ref, owner_ref, cluster_ref, code_ref, old_ref, old_codes_ref,
    coarse_out, codes_out,
    frames_v, mine, theirs, pooled, pool_in, old_v,
    video, videos, into, out_of, amount, meta, metas, both, rows, picks, rest, words, wants, wide, anchors,
    send_c, hop_c, got_c, back_0, back_1, back_2,
    note_0, note_1, note_s, note_2, fresh, fresh_in,
    table, table_1, part, part_2, last, last_in, count, count_in, column,
    load_sem, xs, xr, fs, fr, ps, pr, ns, nr, cs, cr, bs, br, ts, tr, es, er,
):
    dp = lax.axis_index("dp")
    x = lax.axis_index("cent")
    c = lax.rem(dp, 2)
    z = lax.rem(lax.div(dp, 2), NZ)
    y = lax.div(dp, 2 * NZ)
    m = x * 2 + c
    here = (y, z)

    def member(d):
        other = lax.rem(m + d, NL)
        return other, {"dp": (y * NZ + z) * 2 + lax.rem(other, 2), "cent": lax.div(other, 2)}

    def on_y(d):
        other = lax.rem(y + d, NY)
        return other, {"dp": (other * NZ + z) * 2 + c, "cent": x}

    def on_z(d):
        other = lax.rem(z + d, NZ)
        return other, {"dp": (y * NZ + other) * 2 + c, "cent": x}

    on = (on_y, on_z)

    def remote(src, dst, send, recv, target, start=True):
        copy = pltpu.make_async_remote_copy(
            src_ref=src, dst_ref=dst, send_sem=send, recv_sem=recv,
            device_id=target, device_id_type=pl.DeviceIdType.MESH,
        )
        if start:
            copy.start()
        return copy

    def local(src, dst, sem):
        copy = pltpu.make_async_copy(src, dst, sem)
        copy.start()
        return copy

    def wait(copies):
        for copy in copies:
            copy.wait()

    def spread(src, dst, send, recv, stage, axis):
        copies = []
        for d in FAR:
            other, target = on[axis](d)
            copies.append(remote(src(other), dst, send.at[stage, d], recv.at[stage, d], target))
        return copies

    barrier = pltpu.get_barrier_semaphore()
    for d in range(1, 8):
        for find in (member, on_y, on_z):
            pl.semaphore_signal(
                barrier, inc=1, device_id=find(d)[1], device_id_type=pl.DeviceIdType.MESH
            )

    my_lanes = pl.ds(pl.multiple_of(m * W, W), W)
    load = local(frames_ref, frames_v, load_sem.at[0])
    load_mine = local(frames_ref.at[:, my_lanes], theirs.at[m], load_sem.at[1])
    load_old = local(old_ref.at[:, my_lanes], old_v.at[c], load_sem.at[2])

    sub128, lane128 = iota((128, 128), 0), iota((128, 128), 1)
    sub64 = iota((64, 128), 0)
    length = length_ref[...].astype(F32)
    through = hot(sub128 <= lane128)
    before = hot(sub128 < lane128)
    ends_row = dot(jnp.broadcast_to(length, (8, 128)).astype(BF16), through)[0:1]
    ends = columns(ends_row)
    lengths = columns(length)
    starts = ends - lengths
    pieces = []
    for a in range(8):
        position = lane128 + 128.0 * a
        pieces.append(hot(jnp.logical_and(position >= starts, position < ends)))
        meta[16 + a : 17 + a, :] = jnp.sum(
            jnp.where(ends <= position, 1.0, 0.0), axis=0, keepdims=True
        )
    of_video = jnp.concatenate(pieces, axis=1)

    owner_int = owner_ref[...]
    owner = owner_int.astype(F32)
    same = jnp.logical_and(columns(owner) == owner, sub128 < lane128)
    repeat = jnp.sum(jnp.where(same, 1.0, 0.0), axis=0, keepdims=True)
    half = jnp.bitwise_and(owner_int, 1)
    to_y = jnp.right_shift(owner_int, 4)
    to_z = jnp.bitwise_and(jnp.right_shift(owner_int, 1), NZ - 1)
    place = jnp.where(half == 0, to_y * NZ + to_z, to_z * NY + to_y)
    video[0:1, :] = (half * 1024 + place * 16).astype(F32) + repeat
    video[1:2, :] = cluster_ref[...].astype(F32) + 1.0
    video[2:3, :] = place.astype(F32)
    video[3:4, :] = repeat
    video[4:5, :] = half.astype(F32)
    video[5:8, :] = jnp.zeros((3, 128), F32)
    videos[pl.ds(m, 1)] = video[...].reshape(1, 8, 128)

    load.wait()
    for j in range(8):
        part_sum = dot(of_video, frames_v[:, 128 * j : 128 * j + 128])
        pooled[j] = (part_sum / lengths).astype(BF16)
    pl.semaphore_wait(barrier, 21)
    x_copies, f_copies, p_copies = [], [], []
    for d in range(1, 8):
        other, target = member(d)
        x_copies.append(remote(video, videos.at[m], xs.at[0, d], xr.at[0, d], target))
    for d in range(1, 8):
        other, target = member(d)
        p_copies.append(
            remote(pooled.at[other], pool_in.at[m], ps.at[d], pr.at[d], target)
        )
    partner = lax.rem(c + 1, 2)
    old_copy = remote(
        old_ref.at[:, pl.ds(pl.multiple_of((x * 2 + partner) * W, W), W)],
        old_v.at[c], xs.at[0, 0], xr.at[0, 0],
        {"dp": (y * NZ + z) * 2 + partner, "cent": x},
    )
    codes = code_ref[...]
    line_of = jnp.right_shift(codes, 7).astype(F32)
    in_line = jnp.bitwise_and(codes, 127).astype(F32)
    ones = jnp.ones((128, 128), BF16)
    seen = jnp.zeros((64, 128), F32)
    histogram = jnp.zeros((64, 128), F32)
    for a in range(8):
        match = hot(line_of[a : a + 1] == sub64)
        rank = jnp.sum(
            match.astype(F32) * (dot(match, before) + seen), axis=0, keepdims=True
        )
        meta[a : a + 1, :] = line_of[a : a + 1] * 32.0 + rank
        seen = seen + dot(match, ones)
        histogram = histogram + dot_t(match, hot(in_line[a : a + 1] == sub128))
    meta[8:16, :] = in_line
    metas[pl.ds(m, 1)] = meta[...].reshape(1, 24, 128)
    for j in range(8):
        note_0[0, j, 0:8, :] = histogram[8 * j : 8 * j + 8]
        note_0[1, j, 0:8, :] = jnp.zeros((8, 128), F32)

    m_copies = []
    for d in range(1, 8):
        other, target = member(d)
        m_copies.append(remote(meta, metas.at[m], xs.at[1, d], xr.at[1, d], target))
    for d in range(1, 8):
        other, target = member(d)
        lanes = pl.ds(pl.multiple_of(other * W, W), W)
        f_copies.append(
            remote(frames_ref.at[:, lanes], theirs.at[m], fs.at[d], fr.at[d], target)
        )
    pool_in[pl.ds(m, 1)] = pooled[pl.ds(m, 1)]

    wait(x_copies)
    places, values, halves, repeats = [
        [videos[s, i : i + 1, :] for s in range(NL)] for i in (2, 1, 4, 3)
    ]
    note = []
    for h in range(2):
        chosen = [
            jnp.where(
                jnp.logical_and(places[s] == sub64, halves[s] == float(h)), values[s], 0.0
            ).astype(BF16)
            for s in range(NL)
        ]
        lane = [hot(repeats[s] + (here[h] * 16 + 2 * s).astype(F32) == sub128) for s in range(NL)]
        note.append(dot_t(jnp.concatenate(chosen, axis=1), jnp.concatenate(lane, axis=1)))
    for h in range(2):
        for j in range(8):
            note_0[h, j, 8:16, :] = note[h][8 * j : 8 * j + 8]
    n_copies = []
    for h in range(2):
        n_copies += spread(lambda o: note_0.at[h, o], note_1.at[h, here[h]], ns, nr, h, h)
        note_1[h, pl.ds(here[h], 1)] = note_0[h, pl.ds(here[h], 1)]

    wait(p_copies)
    sub256, sub512 = iota((256, 128), 0), iota((512, 128), 0)

    def fill(chunk, carry):
        shift = (chunk * 512).astype(F32)
        pick = jnp.concatenate(
            [hot(videos[s, 0:1, :] + 2.0 * s - shift == sub512) for s in range(NL)], axis=1
        )
        filled = dot(pick, pool_in[...].reshape(1024, W))
        send_c[pl.ds(chunk * 32, 32)] = filled.astype(BF16).reshape(32, 16, W)
        return carry

    lax.fori_loop(0, 4, fill, 0)
    c_copies = []
    for h in range(2):
        c_copies += spread(
            lambda o: send_c.at[pl.ds(64 * h + 8 * o, 8)], hop_c.at[h, here[h]], cs, cr, h, h
        )
        hop_c[h, pl.ds(here[h], 1)] = send_c[pl.ds(64 * h + 8 * here[h], 8)].reshape(1, 8, 16, W)

    wait(n_copies)
    for h in range(2):
        note_s[h] = jnp.sum(note_1[h], axis=0)
    n_copies = []
    for h in range(2):
        n_copies += spread(
            lambda o: note_s.at[h], note_2.at[h, here[1 - h]], ns, nr, 2 + h, 1 - h
        )
        note_2[h, pl.ds(here[1 - h], 1)] = note_s[h].reshape(1, 16, 128)

    def take(d):
        s = lax.rem(m + NL - d, NL)
        for a in range(8):
            both[128 * a : 128 * a + 128, W:] = hot(
                columns(metas[s, 16 + a : 17 + a, :]) == lane128
            )
        both[:, :W] = theirs[s]

        def chunk_of(chunk, carry):
            shift = (chunk * 512).astype(F32)
            pick = jnp.concatenate(
                [hot(metas[s, a : a + 1, :] - shift == sub512) for a in range(8)], axis=1
            )
            out = dot(pick, both[...]).astype(BF16)
            rows[s, pl.ds(chunk * 16, 16)] = out[:, :W].reshape(16, 32, W)
            picks[s, pl.ds(chunk * 16, 16)] = out[:, W:].reshape(16, 32, W)
            return carry

        lax.fori_loop(0, 4, chunk_of, 0)

    def arrive(d):
        if d == 0:
            load_mine.wait()
        else:
            f_copies[d - 1].wait()
        take(d)

    def word(s, carry):
        offset = (lax.rem(s, 4) * 32).astype(F32)
        values, ranks = [], []
        for a in range(8):
            slot = metas[s, a : a + 1, :]
            line = jnp.floor(slot * (1.0 / 32.0))
            rank = slot - 32.0 * line + offset
            value = metas[s, 8 + a : 9 + a, :] + 1.0
            values.append(jnp.where(line == sub64, value, 0.0).astype(BF16))
            ranks.append(hot(rank == sub128))
        total = dot_t(jnp.concatenate(values, axis=1), jnp.concatenate(ranks, axis=1))
        group = pl.ds(lax.div(s, 4), 1)
        words[group] = words[group] + total.reshape(1, 64, 128)
        return carry

    def choose(s, carry):
        info = videos[s]
        wanted = columns(info[3:4] * 128.0 + info[4:5] * 64.0 + info[2:3])
        pick = [hot(wanted == lane128 + 128.0 * t) for t in range(2)]
        wants[pl.ds(s, 1)] = jnp.concatenate(pick, axis=1).reshape(1, 128, 256)
        return carry

    arrive(0)
    wait(m_copies)
    words[...] = jnp.zeros((2, 64, 128), F32)
    lax.fori_loop(0, NL, word, 0)
    lax.fori_loop(0, NL, choose, 0)

    wait(c_copies)
    c_copies = []
    for h in range(2):
        c_copies += spread(
            lambda o: hop_c.at[h, :, o], got_c.at[h, here[1 - h]], cs, cr, 2 + h, 1 - h
        )
        got_c[h, pl.ds(here[1 - h], 1)] = hop_c[h, :, pl.ds(here[1 - h], 1)].reshape(1, 8, 16, W)
    wait(n_copies)
    sub8, lane256 = iota((8, 128), 0), iota((128, 256), 1)
    for h in range(2):
        mask = sub8 == here[1 - h].astype(F32)
        ids = [
            jnp.sum(jnp.where(mask, note_2[h, j, 8:16, :], 0.0), axis=0, keepdims=True)
            for j in range(8)
        ]
        pick = jnp.concatenate([hot(ids[j] == sub256 + 1.0) for j in range(8)], axis=1)
        into[h] = pick
        amount[h] = dot(pick, jnp.ones((1024, W), BF16)) + 1.0
        for j in range(8):
            column_of = columns(ids[j])
            back = jnp.concatenate([column_of, column_of], axis=1) == lane256 + 1.0
            out_of[h, 128 * j : 128 * j + 128, :] = hot(back)
    counts = jnp.zeros((1, 128), F32)
    for j in range(8):
        counts = counts + jnp.sum(
            jnp.where(sub8 == z.astype(F32), note_2[0, j, 0:8, :], 0.0), axis=0, keepdims=True
        )
    count[...] = jnp.broadcast_to(counts, (8, 128))
    count_in[pl.ds(m, 1)] = count[...].reshape(1, 8, 128)
    arrive(1)
    load_old.wait()
    old_copy.wait()
    wait(c_copies)

    b_copies, v_copies, fresh_of = [], [], []
    for h in range(2):
        total = dot(into[h], got_c[h].reshape(1024, W))
        fresh_of.append((total + old_v[h].astype(F32)) / amount[h])
    for h in range(2):
        found = dot(out_of[h], fresh_of[h].astype(BF16)).astype(BF16)
        back_0[h] = found.reshape(8, 8, 16, W)
        b_copies += spread(
            lambda o: back_0.at[h, o], back_1.at[h, here[1 - h]], bs, br, h, 1 - h
        )
        back_1[h, pl.ds(here[1 - h], 1)] = back_0[h, pl.ds(here[1 - h], 1)]
    for h in range(2):
        for q in range(4):
            fresh[2 * q + h] = fresh_of[h][64 * q : 64 * q + 64]
    for d in range(1, 8):
        other, target = member(d)
        v_copies.append(
            remote(fresh.at[other], fresh_in.at[m], es.at[0, d], er.at[0, d], target)
        )
        v_copies.append(
            remote(count, count_in.at[m], es.at[1, d], er.at[1, d], target)
        )
    fresh_in[pl.ds(m, 1)] = fresh[pl.ds(m, 1)]
    arrive(2)
    arrive(3)
    arrive(4)

    wait(b_copies)
    b_copies = []
    for h in range(2):
        b_copies += spread(
            lambda o: back_1.at[h, :, o], back_2.at[h, here[h]], bs, br, 2 + h, h
        )
        back_2[h, pl.ds(here[h], 1)] = back_1[h, :, pl.ds(here[h], 1)].reshape(1, 8, 16, W)
    arrive(5)
    arrive(6)
    arrive(7)
    wait(b_copies)

    wide[...] = back_2[...].reshape(2048, W).astype(F32)
    for s in range(NL):
        found = [wide[pl.ds(2 * s + r, 128, stride=16), :].astype(BF16) for r in range(2)]
        anchors[s] = dot(wants[s], jnp.concatenate(found, axis=0)).astype(BF16)

    def tabulate(to):
        at = pl.ds(to * 8, 8)
        for s in range(NL):
            near = dot(picks[s, at].reshape(256, W), anchors[s])
            left = rows[s, at].reshape(256, W).astype(F32) - near
            rest[:, 32 * s : 32 * s + 32, :] = left.astype(BF16).reshape(8, 32, W)
        low = words[0, pl.ds(pl.multiple_of(to * 8, 8), 8), :]
        high = words[1, pl.ds(pl.multiple_of(to * 8, 8), 8), :]
        for k in range(8):
            pick = jnp.concatenate(
                [hot(w[k : k + 1] == sub128 + 1.0) for w in (low, high)], axis=1
            )
            sums = dot(pick, rest[k]).astype(BF16)
            table[0, pl.ds(to * 8 + k, 1)] = sums[0:64].reshape(1, 64, W)
            table[1, pl.ds(k * 8 + to, 1)] = sums[64:128].reshape(1, 64, W)

    def first_a(d, start):
        other, target = on_y(d)
        return remote(
            table.at[0, pl.ds(8 * other, 8)], table_1.at[0, y], ts.at[0, d], tr.at[0, d],
            target, start,
        )

    def first_b(d, at, size, start):
        other, target = on_z(d)
        return remote(
            table.at[1, pl.ds(8 * other + at, size)], table_1.at[1, z, pl.ds(at, size)],
            ts.at[1, d], tr.at[1, d], target, start,
        )

    def send_group(i, carry):
        far = lax.div(i + 1, 2)
        d = 4 + far - 2 * far * lax.rem(i, 2)
        to = lax.rem(y + d, NY)
        tabulate(to)
        first_a(d, True)
        for e in FAR:
            first_b(e, to, 1, True)
        return carry

    lax.fori_loop(0, 7, send_group, 0)
    tabulate(y)
    for e in FAR:
        first_b(e, y, 1, True)
    for h in range(2):
        table_1[h, pl.ds(here[h], 1)] = table[h, pl.ds(8 * here[h], 8)].reshape(1, 8, 64, W)
    wait(v_copies)
    for s in range(NL):
        coarse_out[:, W * s : W * s + W] = fresh_in[s]
    column[...] = columns(jnp.sum(count_in[...], axis=0)[0:1])
    for d in range(1, 8):
        first_a(d, False).wait()
        first_b(d, 0, 8, False).wait()

    def summed(h, j):
        total = jnp.zeros((64, W), F32)
        for i in range(8):
            total = total + table_1[h, i, pl.ds(j, 1)].reshape(64, W).astype(F32)
        return total.reshape(1, 64, W)

    def second(h, d, start):
        other, target = on[1 - h](d)
        return remote(
            part.at[h, other], part_2.at[h, here[1 - h]], ts.at[2 + h, d], tr.at[2 + h, d],
            target, start,
        )

    def send_sums(i, carry):
        far = lax.div(i + 1, 2)
        d = 4 + far - 2 * far * lax.rem(i, 2)
        for h in range(2):
            j = lax.rem(here[1 - h] + d, 8)
            part[h, pl.ds(j, 1)] = summed(h, j)
            second(h, d, True)
        return carry

    lax.fori_loop(0, 7, send_sums, 0)
    for h in range(2):
        part_2[h, pl.ds(here[1 - h], 1)] = summed(h, here[1 - h])
    for d in range(1, 8):
        for h in range(2):
            second(h, d, False).wait()
    for h in range(2):
        total = jnp.sum(part_2[h], axis=0)
        for q in range(4):
            last[2 * q + h] = total[16 * q : 16 * q + 16]
    e_copies = []
    for d in range(1, 8):
        other, target = member(d)
        e_copies.append(
            remote(last.at[other], last_in.at[m], es.at[2, d], er.at[2, d], target)
        )
    last_in[pl.ds(m, 1)] = last[pl.ds(m, 1)]
    mine[...] = column[pl.ds(pl.multiple_of(c * 64 + x * 16, 16), 16), :] + code_prior
    wait(e_copies)
    for s in range(NL):
        lanes = slice(W * s, W * s + W)
        codes_out[:, lanes] = (last_in[s] + code_prior * old_codes_ref[:, lanes]) / mine[...]


def hand_on(coarse_in, codes_in, coarse_out, codes_out):
    coarse_out[...] = coarse_in[...]
    codes_out[...] = codes_in[...]


def body(frames, video_length, video_owner, video_cluster, frame_code, old_coarse, old_codes):
    dma = pltpu.SemaphoreType.DMA
    vmem = pl.BlockSpec(memory_space=pltpu.VMEM)
    hbm = pl.BlockSpec(memory_space=pl.ANY)
    coarse, codes = pl.pallas_call(
        kernel,
        out_shape=(
            jax.ShapeDtypeStruct((64, 1024), F32),
            jax.ShapeDtypeStruct((16, 1024), F32),
        ),
        in_specs=[hbm, vmem, vmem, vmem, vmem, hbm, vmem],
        out_specs=(vmem, vmem),
        scratch_shapes=[
            pltpu.VMEM((1024, 1024), BF16),
            pltpu.VMEM((16, 128), F32),
            pltpu.VMEM((NL, 1024, W), BF16),
            pltpu.VMEM((NL, 128, W), BF16),
            pltpu.VMEM((NL, 128, W), BF16),
            pltpu.VMEM((2, 256, W), BF16),
            pltpu.VMEM((8, 128), F32),
            pltpu.VMEM((NL, 8, 128), F32),
            pltpu.VMEM((2, 256, 1024), BF16),
            pltpu.VMEM((2, 1024, 256), BF16),
            pltpu.VMEM((2, 256, W), F32),
            pltpu.VMEM((24, 128), F32),
            pltpu.VMEM((NL, 24, 128), F32),
            pltpu.VMEM((1024, 2 * W), BF16),
            pltpu.VMEM((NL, 64, 32, W), BF16),
            pltpu.VMEM((NL, 64, 32, W), BF16),
            pltpu.VMEM((8, 256, W), BF16),
            pltpu.VMEM((2, 64, 128), F32),
            pltpu.VMEM((NL, 128, 256), BF16),
            pltpu.VMEM((2048, W), F32),
            pltpu.VMEM((NL, 128, W), BF16),
            pltpu.VMEM((128, 16, W), BF16),
            pltpu.VMEM((2, 8, 8, 16, W), BF16),
            pltpu.VMEM((2, 8, 8, 16, W), BF16),
            pltpu.VMEM((2, 8, 8, 16, W), BF16),
            pltpu.VMEM((2, 8, 8, 16, W), BF16),
            pltpu.VMEM((2, 8, 8, 16, W), BF16),
            pltpu.VMEM((2, 8, 16, 128), F32),
            pltpu.VMEM((2, 8, 16, 128), F32),
            pltpu.VMEM((2, 16, 128), F32),
            pltpu.VMEM((2, 8, 16, 128), F32),
            pltpu.VMEM((NL, 64, W), F32),
            pltpu.VMEM((NL, 64, W), F32),
            pltpu.VMEM((2, 64, 64, W), BF16),
            pltpu.VMEM((2, 8, 8, 64, W), BF16),
            pltpu.VMEM((2, 8, 64, W), F32),
            pltpu.VMEM((2, 8, 64, W), F32),
            pltpu.VMEM((NL, 16, W), F32),
            pltpu.VMEM((NL, 16, W), F32),
            pltpu.VMEM((8, 128), F32),
            pltpu.VMEM((NL, 8, 128), F32),
            pltpu.VMEM((128, 128), F32),
            dma((3,)),
            dma((2, 8)), dma((2, 8)),
            dma((8,)), dma((8,)),
            dma((8,)), dma((8,)),
            dma((4, 8)), dma((4, 8)),
            dma((4, 8)), dma((4, 8)),
            dma((4, 8)), dma((4, 8)),
            dma((4, 8)), dma((4, 8)),
            dma((3, 8)), dma((3, 8)),
        ],
        compiler_params=pltpu.CompilerParams(
            collective_id=0, has_side_effects=True, vmem_limit_bytes=56 << 20
        ),
    )(
        frames, video_length, video_owner, video_cluster,
        frame_code.reshape(8, 128), old_coarse, old_codes,
    )
    return pl.pallas_call(
        hand_on,
        out_shape=(
            jax.ShapeDtypeStruct((64, 1024), F32),
            jax.ShapeDtypeStruct((16, 1024), F32),
        ),
        in_specs=[vmem, vmem],
        out_specs=(vmem, vmem),
    )(coarse, codes)


def solution(mesh):
    placed = (
        P(("dp", "cent"), None),
        P(("dp", "cent"), None),
        P(("dp", "cent"), None),
        P(("dp", "cent"), None),
        P(("dp", "cent")),
        P("dp", None),
        P(("dp", "cent"), None),
    )
    return jax.shard_map(
        body,
        mesh=mesh,
        in_specs=placed,
        out_specs=(P(("dp", "cent"), None), P(("dp", "cent"), None)),
        check_vma=False,
    )
```

```python
import jax
import jax.numpy as jnp
from jax import lax
from jax.experimental import pallas as pl
from jax.experimental.pallas import tpu as pltpu
from jax.sharding import PartitionSpec as P

code_prior = 16.0
NL = 8
NY = 8
NZ = 8
W = 128
FAR = (4, 3, 5, 2, 6, 1, 7)
F32 = jnp.float32
BF16 = jnp.bfloat16


def iota(shape, dim):
    return lax.broadcasted_iota(jnp.int32, shape, dim).astype(F32)


def hot(condition):
    return jnp.where(condition, 1.0, 0.0).astype(BF16)


def columns(row):
    return jnp.transpose(jnp.broadcast_to(row, (128, 128)))


def dot(a, b):
    return jnp.dot(a, b, preferred_element_type=F32)


def dot_t(a, b):
    return lax.dot_general(a, b, (((1,), (1,)), ((), ())), preferred_element_type=F32)


def kernel(
    frames_ref, length_ref, owner_ref, cluster_ref, code_ref, old_ref, old_codes_ref,
    coarse_out, codes_out,
    frames_v, mine, theirs, pooled, pool_in, old_v,
    video, videos, into, out_of, amount, meta, metas, both, rows, picks, rest, words, wants, wide, anchors,
    send_c, hop_c, got_c, back_0, back_1, back_2,
    note_0, note_1, note_s, note_2, fresh, fresh_in,
    table, table_1, part, part_2, last, last_in, count, count_in, column,
    load_sem, xs, xr, fs, fr, ps, pr, ns, nr, cs, cr, bs, br, ts, tr, es, er,
):
    dp = lax.axis_index("dp")
    x = lax.axis_index("cent")
    c = lax.rem(dp, 2)
    z = lax.rem(lax.div(dp, 2), NZ)
    y = lax.div(dp, 2 * NZ)
    m = x * 2 + c
    here = (y, z)

    def member(d):
        other = lax.rem(m + d, NL)
        return other, {"dp": (y * NZ + z) * 2 + lax.rem(other, 2), "cent": lax.div(other, 2)}

    def on_y(d):
        other = lax.rem(y + d, NY)
        return other, {"dp": (other * NZ + z) * 2 + c, "cent": x}

    def on_z(d):
        other = lax.rem(z + d, NZ)
        return other, {"dp": (y * NZ + other) * 2 + c, "cent": x}

    on = (on_y, on_z)

    def remote(src, dst, send, recv, target, start=True):
        copy = pltpu.make_async_remote_copy(
            src_ref=src, dst_ref=dst, send_sem=send, recv_sem=recv,
            device_id=target, device_id_type=pl.DeviceIdType.MESH,
        )
        if start:
            copy.start()
        return copy

    def local(src, dst, sem):
        copy = pltpu.make_async_copy(src, dst, sem)
        copy.start()
        return copy

    def wait(copies):
        for copy in copies:
            copy.wait()

    def spread(src, dst, send, recv, stage, axis):
        copies = []
        for d in FAR:
            other, target = on[axis](d)
            copies.append(remote(src(other), dst, send.at[stage, d], recv.at[stage, d], target))
        return copies

    barrier = pltpu.get_barrier_semaphore()
    for d in FAR:
        for find in (member, on_y, on_z):
            pl.semaphore_signal(
                barrier, inc=1, device_id=find(d)[1], device_id_type=pl.DeviceIdType.MESH
            )

    my_lanes = pl.ds(pl.multiple_of(m * W, W), W)
    load = local(frames_ref, frames_v, load_sem.at[0])
    load_mine = local(frames_ref.at[:, my_lanes], theirs.at[m], load_sem.at[1])
    load_old = local(old_ref.at[:, my_lanes], old_v.at[c], load_sem.at[2])

    sub128, lane128 = iota((128, 128), 0), iota((128, 128), 1)
    sub64 = iota((64, 128), 0)
    length = length_ref[...].astype(F32)
    through = hot(sub128 <= lane128)
    before = hot(sub128 < lane128)
    ends_row = dot(jnp.broadcast_to(length, (8, 128)).astype(BF16), through)[0:1]
    ends = columns(ends_row)
    lengths = columns(length)
    starts = ends - lengths
    pieces = []
    for a in range(8):
        position = lane128 + 128.0 * a
        pieces.append(hot(jnp.logical_and(position >= starts, position < ends)))
        meta[16 + a : 17 + a, :] = jnp.sum(
            jnp.where(ends <= position, 1.0, 0.0), axis=0, keepdims=True
        )
    of_video = jnp.concatenate(pieces, axis=1)

    owner_int = owner_ref[...]
    owner = owner_int.astype(F32)
    same = jnp.logical_and(columns(owner) == owner, sub128 < lane128)
    repeat = jnp.sum(jnp.where(same, 1.0, 0.0), axis=0, keepdims=True)
    half = jnp.bitwise_and(owner_int, 1)
    to_y = jnp.right_shift(owner_int, 4)
    to_z = jnp.bitwise_and(jnp.right_shift(owner_int, 1), NZ - 1)
    place = jnp.where(half == 0, to_y * NZ + to_z, to_z * NY + to_y)
    video[0:1, :] = (half * 1024 + place * 16).astype(F32) + repeat
    video[1:2, :] = cluster_ref[...].astype(F32) + 1.0
    video[2:3, :] = place.astype(F32)
    video[3:4, :] = repeat
    video[4:5, :] = half.astype(F32)
    video[5:8, :] = jnp.zeros((3, 128), F32)
    videos[pl.ds(m, 1)] = video[...].reshape(1, 8, 128)

    load.wait()
    for j in range(8):
        part_sum = dot(of_video, frames_v[:, 128 * j : 128 * j + 128])
        pooled[j] = (part_sum / lengths).astype(BF16)
    pl.semaphore_wait(barrier, 21)
    x_copies, f_copies, p_copies = [], [], []
    for d in range(1, 8):
        other, target = member(d)
        x_copies.append(remote(video, videos.at[m], xs.at[0, d], xr.at[0, d], target))
    for d in range(1, 8):
        other, target = member(d)
        p_copies.append(
            remote(pooled.at[other], pool_in.at[m], ps.at[d], pr.at[d], target)
        )
    partner = lax.rem(c + 1, 2)
    old_copy = remote(
        old_ref.at[:, pl.ds(pl.multiple_of((x * 2 + partner) * W, W), W)],
        old_v.at[c], xs.at[0, 0], xr.at[0, 0],
        {"dp": (y * NZ + z) * 2 + partner, "cent": x},
    )
    codes = code_ref[...]
    line_of = jnp.right_shift(codes, 7).astype(F32)
    in_line = jnp.bitwise_and(codes, 127).astype(F32)
    ones = jnp.ones((128, 128), BF16)
    seen = jnp.zeros((64, 128), F32)
    histogram = jnp.zeros((64, 128), F32)
    for a in range(8):
        match = hot(line_of[a : a + 1] == sub64)
        rank = jnp.sum(
            match.astype(F32) * (dot(match, before) + seen), axis=0, keepdims=True
        )
        meta[a : a + 1, :] = line_of[a : a + 1] * 32.0 + rank
        seen = seen + dot(match, ones)
        histogram = histogram + dot_t(match, hot(in_line[a : a + 1] == sub128))
    meta[8:16, :] = in_line
    metas[pl.ds(m, 1)] = meta[...].reshape(1, 24, 128)
    for j in range(8):
        note_0[0, j, 0:8, :] = histogram[8 * j : 8 * j + 8]
        note_0[1, j, 0:8, :] = jnp.zeros((8, 128), F32)

    m_copies = []
    for d in range(1, 8):
        other, target = member(d)
        m_copies.append(remote(meta, metas.at[m], xs.at[1, d], xr.at[1, d], target))
    for d in range(1, 8):
        other, target = member(d)
        lanes = pl.ds(pl.multiple_of(other * W, W), W)
        f_copies.append(
            remote(frames_ref.at[:, lanes], theirs.at[m], fs.at[d], fr.at[d], target)
        )
    pool_in[pl.ds(m, 1)] = pooled[pl.ds(m, 1)]

    wait(x_copies)
    places, values, halves, repeats = [
        [videos[s, i : i + 1, :] for s in range(NL)] for i in (2, 1, 4, 3)
    ]
    note = []
    for h in range(2):
        chosen = [
            jnp.where(
                jnp.logical_and(places[s] == sub64, halves[s] == float(h)), values[s], 0.0
            ).astype(BF16)
            for s in range(NL)
        ]
        lane = [hot(repeats[s] + (here[h] * 16 + 2 * s).astype(F32) == sub128) for s in range(NL)]
        note.append(dot_t(jnp.concatenate(chosen, axis=1), jnp.concatenate(lane, axis=1)))
    for h in range(2):
        for j in range(8):
            note_0[h, j, 8:16, :] = note[h][8 * j : 8 * j + 8]
    n_copies = []
    for h in range(2):
        n_copies += spread(lambda o: note_0.at[h, o], note_1.at[h, here[h]], ns, nr, h, h)
        note_1[h, pl.ds(here[h], 1)] = note_0[h, pl.ds(here[h], 1)]

    wait(p_copies)
    sub256, sub512 = iota((256, 128), 0), iota((512, 128), 0)

    def fill(chunk, carry):
        shift = (chunk * 512).astype(F32)
        pick = jnp.concatenate(
            [hot(videos[s, 0:1, :] + 2.0 * s - shift == sub512) for s in range(NL)], axis=1
        )
        filled = dot(pick, pool_in[...].reshape(1024, W))
        send_c[pl.ds(chunk * 32, 32)] = filled.astype(BF16).reshape(32, 16, W)
        return carry

    c_copies = []
    for h in range(2):
        lax.fori_loop(2 * h, 2 * h + 2, fill, 0)
        c_copies += spread(
            lambda o: send_c.at[pl.ds(64 * h + 8 * o, 8)], hop_c.at[h, here[h]], cs, cr, h, h
        )
        hop_c[h, pl.ds(here[h], 1)] = send_c[pl.ds(64 * h + 8 * here[h], 8)].reshape(1, 8, 16, W)

    wait(n_copies)
    for h in range(2):
        note_s[h] = jnp.sum(note_1[h], axis=0)
    n_copies = []
    for h in range(2):
        n_copies += spread(
            lambda o: note_s.at[h], note_2.at[h, here[1 - h]], ns, nr, 2 + h, 1 - h
        )
        note_2[h, pl.ds(here[1 - h], 1)] = note_s[h].reshape(1, 16, 128)

    def take(d):
        s = lax.rem(m + NL - d, NL)
        for a in range(8):
            both[128 * a : 128 * a + 128, W:] = hot(
                columns(metas[s, 16 + a : 17 + a, :]) == lane128
            )
        both[:, :W] = theirs[s]

        def chunk_of(chunk, carry):
            shift = (chunk * 512).astype(F32)
            pick = jnp.concatenate(
                [hot(metas[s, a : a + 1, :] - shift == sub512) for a in range(8)], axis=1
            )
            out = dot(pick, both[...]).astype(BF16)
            rows[s, pl.ds(chunk * 16, 16)] = out[:, :W].reshape(16, 32, W)
            picks[s, pl.ds(chunk * 16, 16)] = out[:, W:].reshape(16, 32, W)
            return carry

        lax.fori_loop(0, 4, chunk_of, 0)

    def arrive(d):
        if d == 0:
            load_mine.wait()
        else:
            f_copies[d - 1].wait()
        take(d)

    def word(s, carry):
        offset = (lax.rem(s, 4) * 32).astype(F32)
        values, ranks = [], []
        for a in range(8):
            slot = metas[s, a : a + 1, :]
            line = jnp.floor(slot * (1.0 / 32.0))
            rank = slot - 32.0 * line + offset
            value = metas[s, 8 + a : 9 + a, :] + 1.0
            values.append(jnp.where(line == sub64, value, 0.0).astype(BF16))
            ranks.append(hot(rank == sub128))
        total = dot_t(jnp.concatenate(values, axis=1), jnp.concatenate(ranks, axis=1))
        group = pl.ds(lax.div(s, 4), 1)
        words[group] = words[group] + total.reshape(1, 64, 128)
        return carry

    def choose(s, carry):
        info = videos[s]
        wanted = columns(info[3:4] * 128.0 + info[4:5] * 64.0 + info[2:3])
        pick = [hot(wanted == lane128 + 128.0 * t) for t in range(2)]
        wants[pl.ds(s, 1)] = jnp.concatenate(pick, axis=1).reshape(1, 128, 256)
        return carry

    arrive(0)
    wait(m_copies)
    words[...] = jnp.zeros((2, 64, 128), F32)
    lax.fori_loop(0, NL, word, 0)
    lax.fori_loop(0, NL, choose, 0)

    wait(c_copies)
    c_copies = []
    for h in range(2):
        c_copies += spread(
            lambda o: hop_c.at[h, :, o], got_c.at[h, here[1 - h]], cs, cr, 2 + h, 1 - h
        )
        got_c[h, pl.ds(here[1 - h], 1)] = hop_c[h, :, pl.ds(here[1 - h], 1)].reshape(1, 8, 16, W)
    wait(n_copies)
    sub8, lane256 = iota((8, 128), 0), iota((128, 256), 1)
    for h in range(2):
        mask = sub8 == here[1 - h].astype(F32)
        ids = [
            jnp.sum(jnp.where(mask, note_2[h, j, 8:16, :], 0.0), axis=0, keepdims=True)
            for j in range(8)
        ]
        pick = jnp.concatenate([hot(ids[j] == sub256 + 1.0) for j in range(8)], axis=1)
        into[h] = pick
        amount[h] = dot(pick, jnp.ones((1024, W), BF16)) + 1.0
        for j in range(8):
            column_of = columns(ids[j])
            back = jnp.concatenate([column_of, column_of], axis=1) == lane256 + 1.0
            out_of[h, 128 * j : 128 * j + 128, :] = hot(back)
    counts = jnp.zeros((1, 128), F32)
    for j in range(8):
        counts = counts + jnp.sum(
            jnp.where(sub8 == z.astype(F32), note_2[0, j, 0:8, :], 0.0), axis=0, keepdims=True
        )
    count[...] = jnp.broadcast_to(counts, (8, 128))
    count_in[pl.ds(m, 1)] = count[...].reshape(1, 8, 128)
    arrive(1)
    load_old.wait()
    old_copy.wait()
    wait(c_copies)

    b_copies, v_copies, fresh_of = [], [], []
    for h in range(2):
        total = dot(into[h], got_c[h].reshape(1024, W))
        fresh_of.append((total + old_v[h].astype(F32)) / amount[h])
    for h in range(2):
        found = dot(out_of[h], fresh_of[h].astype(BF16)).astype(BF16)
        back_0[h] = found.reshape(8, 8, 16, W)
        b_copies += spread(
            lambda o: back_0.at[h, o], back_1.at[h, here[1 - h]], bs, br, h, 1 - h
        )
        back_1[h, pl.ds(here[1 - h], 1)] = back_0[h, pl.ds(here[1 - h], 1)]
    for h in range(2):
        for q in range(4):
            fresh[2 * q + h] = fresh_of[h][64 * q : 64 * q + 64]
    for d in range(1, 8):
        other, target = member(d)
        v_copies.append(
            remote(fresh.at[other], fresh_in.at[m], es.at[0, d], er.at[0, d], target)
        )
        v_copies.append(
            remote(count, count_in.at[m], es.at[1, d], er.at[1, d], target)
        )
    fresh_in[pl.ds(m, 1)] = fresh[pl.ds(m, 1)]
    arrive(2)
    arrive(3)
    arrive(4)

    wait(b_copies)
    b_copies = []
    for h in range(2):
        b_copies += spread(
            lambda o: back_1.at[h, :, o], back_2.at[h, here[h]], bs, br, 2 + h, h
        )
        back_2[h, pl.ds(here[h], 1)] = back_1[h, :, pl.ds(here[h], 1)].reshape(1, 8, 16, W)
    arrive(5)
    arrive(6)
    arrive(7)
    wait(b_copies)

    wide[...] = back_2[...].reshape(2048, W).astype(F32)
    for s in range(NL):
        found = [wide[pl.ds(2 * s + r, 128, stride=16), :].astype(BF16) for r in range(2)]
        anchors[s] = dot(wants[s], jnp.concatenate(found, axis=0)).astype(BF16)

    def tabulate(to):
        at = pl.ds(to * 8, 8)
        for s in range(NL):
            near = dot(picks[s, at].reshape(256, W), anchors[s])
            left = rows[s, at].reshape(256, W).astype(F32) - near
            rest[:, 32 * s : 32 * s + 32, :] = left.astype(BF16).reshape(8, 32, W)
        low = words[0, pl.ds(pl.multiple_of(to * 8, 8), 8), :]
        high = words[1, pl.ds(pl.multiple_of(to * 8, 8), 8), :]
        for k in range(8):
            pick = jnp.concatenate(
                [hot(w[k : k + 1] == sub128 + 1.0) for w in (low, high)], axis=1
            )
            sums = dot(pick, rest[k]).astype(BF16)
            table[0, pl.ds(to * 8 + k, 1)] = sums[0:64].reshape(1, 64, W)
            table[1, pl.ds(k * 8 + to, 1)] = sums[64:128].reshape(1, 64, W)

    def first_a(d, start):
        other, target = on_y(d)
        return remote(
            table.at[0, pl.ds(8 * other, 8)], table_1.at[0, y], ts.at[0, d], tr.at[0, d],
            target, start,
        )

    def first_b(d, at, size, start):
        other, target = on_z(d)
        return remote(
            table.at[1, pl.ds(8 * other + at, size)], table_1.at[1, z, pl.ds(at, size)],
            ts.at[1, d], tr.at[1, d], target, start,
        )

    def send_group(i, carry):
        far = lax.div(i + 1, 2)
        d = 4 + far - 2 * far * lax.rem(i, 2)
        to = lax.rem(y + d, NY)
        tabulate(to)
        first_a(d, True)
        for e in FAR:
            first_b(e, to, 1, True)
        return carry

    lax.fori_loop(0, 7, send_group, 0)
    tabulate(y)
    for e in FAR:
        first_b(e, y, 1, True)
    for h in range(2):
        table_1[h, pl.ds(here[h], 1)] = table[h, pl.ds(8 * here[h], 8)].reshape(1, 8, 64, W)
    wait(v_copies)
    for s in range(NL):
        coarse_out[:, W * s : W * s + W] = fresh_in[s]
    column[...] = columns(jnp.sum(count_in[...], axis=0)[0:1])
    for d in range(1, 8):
        first_a(d, False).wait()
        first_b(d, 0, 8, False).wait()

    def summed(h, j):
        total = jnp.zeros((64, W), F32)
        for i in range(8):
            total = total + table_1[h, i, pl.ds(j, 1)].reshape(64, W).astype(F32)
        return total.reshape(1, 64, W)

    def second(h, d, start):
        other, target = on[1 - h](d)
        return remote(
            part.at[h, other], part_2.at[h, here[1 - h]], ts.at[2 + h, d], tr.at[2 + h, d],
            target, start,
        )

    def send_sums(i, carry):
        far = lax.div(i + 1, 2)
        d = 4 + far - 2 * far * lax.rem(i, 2)
        for h in range(2):
            j = lax.rem(here[1 - h] + d, 8)
            part[h, pl.ds(j, 1)] = summed(h, j)
            second(h, d, True)
        return carry

    lax.fori_loop(0, 7, send_sums, 0)
    for h in range(2):
        part_2[h, pl.ds(here[1 - h], 1)] = summed(h, here[1 - h])
    for d in range(1, 8):
        for h in range(2):
            second(h, d, False).wait()
    for h in range(2):
        total = jnp.sum(part_2[h], axis=0)
        for q in range(4):
            last[2 * q + h] = total[16 * q : 16 * q + 16]
    e_copies = []
    for d in range(1, 8):
        other, target = member(d)
        e_copies.append(
            remote(last.at[other], last_in.at[m], es.at[2, d], er.at[2, d], target)
        )
    last_in[pl.ds(m, 1)] = last[pl.ds(m, 1)]
    mine[...] = column[pl.ds(pl.multiple_of(c * 64 + x * 16, 16), 16), :] + code_prior
    wait(e_copies)
    for s in range(NL):
        lanes = slice(W * s, W * s + W)
        codes_out[:, lanes] = (last_in[s] + code_prior * old_codes_ref[:, lanes]) / mine[...]


def hand_on(coarse_in, codes_in, coarse_out, codes_out):
    coarse_out[...] = coarse_in[...]
    codes_out[...] = codes_in[...]


def body(frames, video_length, video_owner, video_cluster, frame_code, old_coarse, old_codes):
    dma = pltpu.SemaphoreType.DMA
    vmem = pl.BlockSpec(memory_space=pltpu.VMEM)
    hbm = pl.BlockSpec(memory_space=pl.ANY)
    coarse, codes = pl.pallas_call(
        kernel,
        out_shape=(
            jax.ShapeDtypeStruct((64, 1024), F32),
            jax.ShapeDtypeStruct((16, 1024), F32),
        ),
        in_specs=[hbm, vmem, vmem, vmem, vmem, hbm, vmem],
        out_specs=(vmem, vmem),
        scratch_shapes=[
            pltpu.VMEM((1024, 1024), BF16),
            pltpu.VMEM((16, 128), F32),
            pltpu.VMEM((NL, 1024, W), BF16),
            pltpu.VMEM((NL, 128, W), BF16),
            pltpu.VMEM((NL, 128, W), BF16),
            pltpu.VMEM((2, 256, W), BF16),
            pltpu.VMEM((8, 128), F32),
            pltpu.VMEM((NL, 8, 128), F32),
            pltpu.VMEM((2, 256, 1024), BF16),
            pltpu.VMEM((2, 1024, 256), BF16),
            pltpu.VMEM((2, 256, W), F32),
            pltpu.VMEM((24, 128), F32),
            pltpu.VMEM((NL, 24, 128), F32),
            pltpu.VMEM((1024, 2 * W), BF16),
            pltpu.VMEM((NL, 64, 32, W), BF16),
            pltpu.VMEM((NL, 64, 32, W), BF16),
            pltpu.VMEM((8, 256, W), BF16),
            pltpu.VMEM((2, 64, 128), F32),
            pltpu.VMEM((NL, 128, 256), BF16),
            pltpu.VMEM((2048, W), F32),
            pltpu.VMEM((NL, 128, W), BF16),
            pltpu.VMEM((128, 16, W), BF16),
            pltpu.VMEM((2, 8, 8, 16, W), BF16),
            pltpu.VMEM((2, 8, 8, 16, W), BF16),
            pltpu.VMEM((2, 8, 8, 16, W), BF16),
            pltpu.VMEM((2, 8, 8, 16, W), BF16),
            pltpu.VMEM((2, 8, 8, 16, W), BF16),
            pltpu.VMEM((2, 8, 16, 128), F32),
            pltpu.VMEM((2, 8, 16, 128), F32),
            pltpu.VMEM((2, 16, 128), F32),
            pltpu.VMEM((2, 8, 16, 128), F32),
            pltpu.VMEM((NL, 64, W), F32),
            pltpu.VMEM((NL, 64, W), F32),
            pltpu.VMEM((2, 64, 64, W), BF16),
            pltpu.VMEM((2, 8, 8, 64, W), BF16),
            pltpu.VMEM((2, 8, 64, W), F32),
            pltpu.VMEM((2, 8, 64, W), F32),
            pltpu.VMEM((NL, 16, W), F32),
            pltpu.VMEM((NL, 16, W), F32),
            pltpu.VMEM((8, 128), F32),
            pltpu.VMEM((NL, 8, 128), F32),
            pltpu.VMEM((128, 128), F32),
            dma((3,)),
            dma((2, 8)), dma((2, 8)),
            dma((8,)), dma((8,)),
            dma((8,)), dma((8,)),
            dma((4, 8)), dma((4, 8)),
            dma((4, 8)), dma((4, 8)),
            dma((4, 8)), dma((4, 8)),
            dma((4, 8)), dma((4, 8)),
            dma((3, 8)), dma((3, 8)),
        ],
        compiler_params=pltpu.CompilerParams(
            collective_id=0, has_side_effects=True, vmem_limit_bytes=56 << 20
        ),
    )(
        frames, video_length, video_owner, video_cluster,
        frame_code.reshape(8, 128), old_coarse, old_codes,
    )
    return pl.pallas_call(
        hand_on,
        out_shape=(
            jax.ShapeDtypeStruct((64, 1024), F32),
            jax.ShapeDtypeStruct((16, 1024), F32),
        ),
        in_specs=[vmem, vmem],
        out_specs=(vmem, vmem),
    )(coarse, codes)


def solution(mesh):
    placed = (
        P(("dp", "cent"), None),
        P(("dp", "cent"), None),
        P(("dp", "cent"), None),
        P(("dp", "cent"), None),
        P(("dp", "cent")),
        P("dp", None),
        P(("dp", "cent"), None),
    )
    return jax.shard_map(
        body,
        mesh=mesh,
        in_specs=placed,
        out_specs=(P(("dp", "cent"), None), P(("dp", "cent"), None)),
        check_vma=False,
    )
```
